256 devices in a mesh: dp: 4 (over y), blocks: 64 (over x, z, core).
Axes of the slice: x: 4, y: 4, z: 8, core: 2. Of those that a mesh axis runs over, the one named last changes fastest.
Arguments:
- tokens: bfloat16 [16384, 8192], P('blocks', 'dp'), may hold values from -6 to 6
- dec_bias: float32 [8192], P('dp'), may hold values from -3 to 3
- routes: int32 [16384, 2], P('blocks'), may hold values from 0 to 63, all different within a row; in each aligned block of 256 rows (0 to 255, 256 to 511, ...) at most 16 rows name the same one
- latent_picks: int32 [16384, 2, 16], P('blocks'), may hold values from 0 to 1023
- enc_weight: bfloat16 [64, 8192, 1024], P('blocks', 'dp'), may hold values from -0.0625 to 0.0625
- dec_weight: bfloat16 [64, 1024, 8192], P('blocks', None, 'dp'), may hold values from -1 to 1
- enc_bias: float32 [64, 1024], P('blocks'), may hold values from -3 to 3
Outputs:
- reconstruction: bfloat16 [16384, 8192], P('blocks', 'dp')
The draws below stay inside these ranges and needn't reach their ends.
Inputs may be any that keep to these rules, and one draw needn't show every extreme that they name: `routes`: each row names 2 different blocks; among the rows of one index of blocks no block is named by more than 16 rows, and some block by exactly 16. `latent_picks`: indices within a block; a row may name an index more than once.
All inputs are finite; a program needn't handle non-finite values.
Results may differ from the reference program's by a relative error of at most 0.0059.
Values may be sent and summed in bfloat16 or wider, within the bound.
A program may use at most 64 MiB of HBM per device.

```python
import math
import jax
import jax.numpy as jnp
import numpy as np
from jax import lax

D = 8192
LAT = 1024
K_BLK = 2
KIN = 16
R = 256
NBLK = 64
CAP = 16
TOKENS = 16384


def plant(entries, own_key, low, largest):
    longest = entries.shape.index(max(entries.shape))
    spots = []
    for shift in (0, 1):
        where = [jax.random.randint(jax.random.fold_in(own_key, axis), (), 0, length) for axis, length in enumerate(entries.shape)]
        where[longest] = (where[longest] + shift) % entries.shape[longest]
        spots.append(tuple(where))
    return entries.at[spots[0]].set(low).at[spots[1]].set(largest)


def shard_levels(key, shape, split, low, top_value):
    factor_of, own = 1.0, jax.random.fold_in(key, 6)
    for dim, shards_of in split:
        draws = jnp.exp(jax.random.uniform(jax.random.fold_in(own, dim), (shards_of,), jnp.float32, low / len(split), top_value / len(split)))
        factor_of = factor_of * jnp.repeat(draws, shape[dim] // shards_of).reshape([-1 if axis == dim else 1 for axis in range(len(shape))])
    return factor_of


def routed_block(own_key, own, number, rows, amount, top, most, skew):
    order = jax.random.permutation(own_key, amount)
    heavy_load, usual = load_shares(amount, rows * top, most, skew, True), load_shares(amount, rows * top, most, skew, False)
    places = jnp.arange(amount)

    def named(tallies, offset_by):
        used = int((tallies > 0).sum())
        fixed = max(1, used // 4)
        moved = fixed + (places - fixed + offset_by * (used - fixed)) % max(1, amount - fixed)
        return jnp.zeros((amount,), jnp.int32).at[order[jnp.where(places < fixed, places, moved)]].set(jnp.asarray(tallies, jnp.int32))

    tallies = jnp.where(number % 4 == 0, named(heavy_load, number // 4), named(usual, number - number // 4 - 1))
    mixed = jax.random.permutation(jax.random.fold_in(own, 3), amount)
    giver, receiver = mixed[0:amount // 2 * 2:2], mixed[1:amount // 2 * 2:2]
    margin = jnp.minimum(tallies[giver] - 1, most - tallies[receiver]) // 2
    margin = jnp.where((giver == order[0]) | (receiver == order[0]) | (tallies[receiver] == 0), 0, jnp.maximum(margin, 0))
    moved = jax.random.randint(jax.random.fold_in(own, 4), (amount // 2,), 0, 1 << 20) % (margin + 1)
    tallies = tallies.at[giver].add(-moved).at[receiver].add(moved)
    labels = jnp.searchsorted(jnp.cumsum(tallies), jnp.arange(rows * top), side="right").astype(jnp.int32)
    table = labels.reshape(top, rows).T
    table = table[jax.random.permutation(jax.random.fold_in(own, 1), rows)]
    offset_by = jax.random.randint(jax.random.fold_in(own, 2), (rows, 1), 0, top)
    return jnp.take_along_axis(table, (jnp.arange(top)[None, :] + offset_by) % top, axis=1)


def load_shares(amount, total, most, lean, full):
    weights = [(1 << 20) // math.isqrt(grade ** lean) + 1 for grade in range(1, amount + 1)]
    largest = most if full else min(most, max(-(-total // amount), total * weights[0] // sum(weights)))
    least = 1 if total - largest >= amount - 1 else 0
    counts, spare = [largest] + [least] * (amount - 1), total - largest - least * (amount - 1)
    while spare > 0:
        movable = [i for i in range(1, amount) if counts[i] < largest] or [i for i in range(1, amount) if counts[i] < most]
        mass, budget = sum([weights[i] for i in movable]), spare
        for i in movable:
            extra = min(most - counts[i], max(1, budget * weights[i] // mass), spare)
            counts[i] = counts[i] + extra
            spare = spare - extra
    return np.array(counts)


def normal_values(stream_key, shape, deviation, bound, shards=(), held_as=jnp.bfloat16):
    values = jax.random.normal(stream_key, shape, jnp.float32) * deviation
    if len(shards) > 0:
        values = shard_levels(stream_key, shape, shards, -0.22, 0.18) * values
    return jnp.clip(values, min=-bound, max=bound).astype(held_as)


def setup_inputs(seed: int = 0) -> dict:
    splits = jax.random.split(jax.random.key(seed), 8)
    tokens = normal_values(splits[0], (TOKENS, D), 1.0, 6.0, ((0, 64), (1, 4)))
    dec_bias = normal_values(splits[1], (D,), 0.5, 3.0, ((0, 4),), jnp.float32)
    routes_keys = jax.random.split(jax.random.fold_in(splits[2], 1), TOKENS // R)
    routes_turns = jax.random.permutation(jax.random.fold_in(splits[2], 3), TOKENS // R)
    routes = jax.vmap(lambda own, number: routed_block(jax.random.fold_in(splits[2], 2), own, number, R, NBLK, K_BLK, CAP, 2))(routes_keys, routes_turns).reshape((TOKENS, K_BLK))
    latent_picks = plant(jax.random.randint(splits[3], (TOKENS, K_BLK, KIN), 0, LAT), jax.random.fold_in(splits[3], 1), 0, LAT - 1).astype(jnp.int32)
    enc_weight = normal_values(splits[4], (NBLK, D, LAT), D ** -0.5, 0.0625, ((0, 64), (1, 4)))
    dec_weight = normal_values(splits[5], (NBLK, LAT, D), (2 * KIN) ** -0.5, 1.0, ((0, 64), (2, 4)))
    enc_bias = normal_values(splits[6], (NBLK, LAT), 0.5, 3.0, ((0, 64),), jnp.float32)
    return {"tokens": tokens, "dec_bias": dec_bias, "routes": routes, "latent_picks": latent_picks, "enc_weight": enc_weight, "dec_weight": dec_weight, "enc_bias": enc_bias}


def reference(tokens, dec_bias, routes, latent_picks, enc_weight, dec_weight, enc_bias):
    centered = (tokens.astype(jnp.float32) - dec_bias).astype(jnp.bfloat16)
    tile_rows = math.gcd(TOKENS, 64)
    tile_count = TOKENS // tile_rows
    pair_count = tile_rows * K_BLK
    earlier = jnp.tril(jnp.ones((KIN, KIN), jnp.int32), -1) > 0

    def one_tile(index):
        first = (index * tile_rows).astype(jnp.int32)
        block_rows = lax.dynamic_slice_in_dim(centered, first, tile_rows, 0)
        owners = lax.dynamic_slice_in_dim(routes, first, tile_rows, 0).reshape(pair_count)
        chosen = lax.dynamic_slice_in_dim(latent_picks, first, tile_rows, 0).reshape(pair_count, KIN)
        repeated = jnp.repeat(block_rows, K_BLK, axis=0)
        columns = enc_weight[owners[:, None], :, chosen]
        pre = jnp.einsum("pkd,pd->pk", columns.astype(jnp.float32), repeated.astype(jnp.float32))
        pre = pre + enc_bias[owners[:, None], chosen]
        repeat_mask = jnp.any((chosen[:, :, None] == chosen[:, None, :]) & earlier[None], axis=2)
        active = jnp.where(repeat_mask, 0.0, jnp.maximum(pre, 0.0)).astype(jnp.bfloat16)
        active = lax.optimization_barrier(active).astype(jnp.float32)
        dec_rows = dec_weight[owners[:, None], chosen, :]
        partial_value = jnp.einsum("pk,pkd->pd", active, dec_rows.astype(jnp.float32)).astype(jnp.bfloat16)
        partial_value = lax.optimization_barrier(partial_value).astype(jnp.float32)
        summed = partial_value.reshape(tile_rows, K_BLK, D).sum(axis=1) + dec_bias
        return summed.astype(jnp.bfloat16)

    result = lax.map(one_tile, jnp.arange(tile_count, dtype=jnp.int32))
    return result.reshape(TOKENS, D)
```

```python
import functools

import jax
import jax.numpy as jnp
from jax import lax
from jax.experimental import pallas as pl
from jax.experimental.pallas import tpu as pltpu
from jax.sharding import PartitionSpec as P

F32 = jnp.float32
BF16 = jnp.bfloat16
MESH = pl.DeviceIdType.MESH
RING = 8
CORES = 2
CAP = 16
CHUNKS = 8


def dot(a, b):
    return jnp.dot(a, b, preferred_element_type=F32)


def iota(shape, axis):
    return lax.broadcasted_iota(jnp.int32, shape, axis)


def kernel(
    tok, dbias, routes, picks, ebias, enc_hbm, dec_hbm, out,
    enc, dec, cen, r1, r2, s3, r3, r4, xsa, xsb, xra, xrb, acc_a, acc_b, act_a, act_b,
    ysa, ysb, yra, yrb, b4, b3, b2, b1, t4, t3, t2, t1,
    pown, pone, ptwo, tpown, tpone, tptwo,
    tgt, tgt1, tgt2, meta, m1, m2, m3s, m3, m4, ms, mr, idx_a, idx_b,
    ya, yb, yar, ybr,
    wsem, hs, hq, us, uq, xs_sem, xq_sem, xl_sem, vs_sem, vq_sem, vl_sem,
    ms_sem, mq_sem, mx_sem, ysem_s, ysem_q,
):
    rows = tok.shape[0]
    F, _, C = cen.shape
    NP = xsa.shape[1]
    NS = NP * CAP
    HALF = NS // 2
    GA, GB = xsa.shape[2] // CAP, xsb.shape[2] // CAP
    top = routes.shape[1]
    lat = enc.shape[1]
    Y = lax.axis_size("dp")

    y = lax.axis_index("dp")
    b = lax.axis_index("blocks")
    core = lax.rem(b, CORES)
    z = lax.rem(lax.div(b, CORES), RING)
    x = lax.div(b, CORES * RING)
    me = x * CORES + core

    def block_of(p, plane):
        return (lax.div(p, CORES) * RING + plane) * CORES + lax.rem(p, CORES)

    def plane_of(step):
        return lax.rem(z + step + RING, RING)

    ahead = (block_of(me, plane_of(1)), block_of(me, plane_of(-1)))

    def to_peer(turn):
        p = lax.rem(me + turn, NP)
        return p, (y, block_of(p, z))

    def z_copy(src, dst, ssem, rsem, way):
        return pltpu.make_async_remote_copy(
            src_ref=src, dst_ref=dst, send_sem=ssem, recv_sem=rsem,
            device_id=(y, ahead[way]), device_id_type=MESH,
        )

    barrier = pltpu.get_barrier_semaphore()
    for way in range(2):
        pl.semaphore_signal(barrier, inc=1, device_id=(y, ahead[way]), device_id_type=MESH)
    for turn in range(1, NP):
        pl.semaphore_signal(barrier, inc=1, device_id=to_peer(turn)[1], device_id_type=MESH)
    for turn in range(1, Y):
        pl.semaphore_signal(
            barrier, inc=1, device_id=(lax.rem(y + turn, Y), b), device_id_type=MESH
        )
    enc_copy = pltpu.make_async_copy(enc_hbm.at[0], enc, wsem.at[0])
    dec_copy = pltpu.make_async_copy(dec_hbm.at[0], dec, wsem.at[1])
    enc_copy.start()
    dec_copy.start()
    pl.semaphore_wait(barrier, 2 + NP - 1 + Y - 1)

    def hop(h, w, f):
        src, dst = (
            (cen.at[f], r1.at[w, f]),
            (r1.at[w, f], r2.at[w, f]),
            (s3.at[w, f], r3.at[w, f]),
            (r3.at[w, f, pl.ds(NS, HALF)], r4.at[w, f]),
        )[h]
        return z_copy(src, dst, hs.at[h, w, f], hq.at[h, w, f], w)

    def back(h, w, f):
        src, dst = (
            (b1.at[w, f], t1.at[w, f]),
            (b2.at[w, f], t2.at[w, f]),
            (b3.at[w, f], t3.at[w, f]),
            (b4.at[w, f], t4.at[w, f]),
        )[h]
        return z_copy(src, dst, us.at[h, w, f], uq.at[h, w, f], 1 - w)

    def meta_hop(h, w):
        src, dst = (
            (meta, m1.at[w]),
            (m1.at[w], m2.at[w]),
            (m3s.at[w], m3.at[w]),
            (m3.at[w, pl.ds(NS, HALF)], m4.at[w]),
        )[h]
        return z_copy(src, dst, ms_sem.at[h, w], mq_sem.at[h, w], w)

    def tgt_hop(h, w):
        src, dst = ((tgt, tgt1.at[w]), (tgt1.at[w], tgt2.at[w]))[h]
        return z_copy(src, dst, ms_sem.at[4 + h, w], mq_sem.at[4 + h, w], w)

    class Exchange:
        def __init__(self, send, recv, ssem, rsem, lsem):
            self.send, self.recv, self.sems = send, recv, (ssem, rsem, lsem)

        def start(self):
            for turn in range(1, NP):
                p, device = to_peer(turn)
                pltpu.make_async_remote_copy(
                    src_ref=self.send.at[p], dst_ref=self.recv.at[me],
                    send_sem=self.sems[0], recv_sem=self.sems[1],
                    device_id=device, device_id_type=MESH,
                ).start()
            self.local().start()

        def local(self):
            return pltpu.make_async_copy(self.send.at[me], self.recv.at[me], self.sems[2])

        def both(self):
            return pltpu.make_async_remote_copy(
                src_ref=self.send.at[pl.ds(0, NP - 1)], dst_ref=self.recv.at[pl.ds(0, NP - 1)],
                send_sem=self.sems[0], recv_sem=self.sems[1],
                device_id=to_peer(1)[1], device_id_type=MESH,
            )

        def wait_recv(self):
            self.both().wait_recv()
            self.local().wait()

        def wait_send(self):
            self.both().wait_send()

    def out_a(f):
        return Exchange(xsa.at[f], xra.at[f], xs_sem.at[0, f], xq_sem.at[0, f], xl_sem.at[0, f])

    def out_b(f):
        return Exchange(xsb.at[f], xrb.at[f], xs_sem.at[1, f], xq_sem.at[1, f], xl_sem.at[1, f])

    def home_a(f):
        return Exchange(ysa.at[f], yra.at[f], vs_sem.at[0, f], vq_sem.at[0, f], vl_sem.at[0, f])

    def home_b(f):
        return Exchange(ysb.at[f], yrb.at[f], vs_sem.at[1, f], vq_sem.at[1, f], vl_sem.at[1, f])

    meta_x = Exchange(ms, mr, mx_sem.at[0], mx_sem.at[1], mx_sem.at[2])

    def y_copy(turn, src, dst, which):
        return pltpu.make_async_remote_copy(
            src_ref=src, dst_ref=dst.at[turn - 1],
            send_sem=ysem_s.at[which, turn - 1], recv_sem=ysem_q.at[which, turn - 1],
            device_id=(lax.rem(y + turn, Y), b), device_id_type=MESH,
        )

    def placing(targets, plane, first, count):
        q = iota((count, rows), 0) + first
        ids = ((lax.shift_right_logical(q, 5) * RING + plane) * CORES
               + (lax.shift_right_logical(q, 4) & 1)) * CAP + (q & (CAP - 1))
        ids = ids.astype(F32)
        return [jnp.where(targets[k:k + 1, :] == ids, 1.0, 0.0) for k in range(top)]

    def put(p_ref, t_ref, lo, kinds):
        whole = kinds[0]
        for other in kinds[1:]:
            whole = whole + other
        n = whole.shape[0]
        p_ref[lo:lo + n, :] = whole.astype(BF16)
        t_ref[:, lo:lo + n] = whole.T.astype(BF16)

    def pick_rows(kinds, source):
        total = None
        for k, one in enumerate(kinds):
            part = dot(one.astype(BF16), source).astype(BF16)
            take = (iota((128, 128), 0) == iota((128, 128), 1) + 32 * k) & (iota((128, 128), 1) < 32)
            part = dot(part, jnp.where(take, 1.0, 0.0).astype(BF16))
            total = part if total is None else total + part
        return total.astype(BF16)

    def to_peers(ref, g, value):
        ref[:, g * CAP:(g + 1) * CAP, :] = value.reshape(NP, CAP, value.shape[-1])

    def build_meta():
        lane = iota((rows, 128), 1)
        before = jnp.where(iota((rows, rows), 0) > iota((rows, rows), 1), 1.0, 0.0).astype(BF16)
        so_far = jnp.zeros((1, 128), F32)
        spread = jnp.zeros((rows, 128), F32)
        for k in range(top):
            owner = routes[:, k:k + 1]
            named = jnp.where(owner == lane, 1.0, 0.0)
            rank = jnp.sum(named * (dot(before, named.astype(BF16)) + so_far), axis=1, keepdims=True)
            so_far = so_far + jnp.sum(named, axis=0, keepdims=True)
            spread = jnp.where(lane == k, owner.astype(F32) * CAP + rank, spread)
        tgt[...] = spread.T[0:8, :]
        chosen = picks[...]
        n = chosen.shape[1]
        col, lane = iota((n, 128), 0), iota((n, 128), 1)
        base = lax.shift_right_logical(col, 4) * 32 + (col & 15)
        hi = lax.shift_right_logical(chosen, 3).astype(F32).astype(BF16)
        lo = (chosen & 7).astype(F32).astype(BF16)
        meta[...] = (
            dot(hi, jnp.where(lane == base, 1.0, 0.0).astype(BF16))
            + dot(lo, jnp.where(lane == base + 16, 1.0, 0.0).astype(BF16))
        ).astype(BF16)

    def pick_values(acc, idx, count, send):
        @pl.loop(0, count)
        def _(j):
            at = pl.ds(pl.multiple_of(j * 128, 128), 128)
            ids = idx[at, :]
            got = jnp.zeros((128, 128), F32)
            for tile in range(lat // 128):
                here = jnp.take_along_axis(
                    acc[at, tile * 128:(tile + 1) * 128], ids & 127, axis=1,
                    mode="promise_in_bounds",
                )
                got = jnp.where(lax.shift_right_logical(ids, 7) == tile, here, got)
            send[pl.ds(pl.multiple_of(j * CAP, CAP), CAP), :] = got.T[0:CAP, :]

    def spread_values(send, recv, idx, count, act):
        @pl.loop(0, count)
        def _(j):
            at = pl.ds(pl.multiple_of(j * 128, 128), 128)
            small = pl.ds(pl.multiple_of(j * CAP, CAP), CAP)
            value = send[small, :]
            for turn in range(1, Y):
                value = value + recv[turn - 1, small, :]
            value = jnp.maximum(value, 0.0)
            value = jnp.concatenate([value, jnp.zeros((128 - CAP, 128), F32)], axis=0).T
            ids = idx[at, :]
            lane = iota((32, lat), 1)
            for part in range(4):
                sub = slice(part * 32, (part + 1) * 32)
                full = jnp.zeros((32, lat), F32)
                for i in range(CAP):
                    full = jnp.where(lane == ids[sub, i:i + 1], value[sub, i:i + 1], full)
                act[pl.ds(pl.multiple_of(j * 128 + part * 32, 32), 32), :] = full.astype(BF16)

    def read_picks(mr_lo, mr_hi, idx):
        n = idx.shape[0]
        one = mr[:, mr_lo * CAP:mr_hi * CAP, :].reshape(n, 128)
        j, i = iota((128, 128), 0), iota((128, 128), 1)
        weigh = jnp.where(j == i, 8.0, jnp.where(j == i + 16, 1.0, 0.0))
        weigh = jnp.where(i < 16, weigh, 0.0).astype(BF16)
        idx[...] = dot(one, weigh).astype(jnp.int32)

    def encode(acc, value, f):
        at = pl.ds(pl.multiple_of(f * C, C), C)
        width = min(lat, 256)

        @pl.loop(0, lat // width)
        def _(n):
            cols = pl.ds(pl.multiple_of(n * width, width), width)
            acc[:, cols] += dot(value, enc[at, cols])

    def decode(act, ref, f):
        at = pl.ds(pl.multiple_of(f * C, C), C)
        value = dot(act[...], dec[:, at]).astype(BF16)
        ref[...] = value.reshape(NP, value.shape[0] // NP, C)

    scale = jnp.where(y == 0, 1.0, 0.0)
    acc_a[...] = jnp.broadcast_to(ebias[...] * scale, acc_a.shape)
    acc_b[...] = jnp.broadcast_to(ebias[...] * scale, acc_b.shape)

    @pl.loop(0, F + 5)
    def _(k):
        @pl.when(k < F)
        def _():
            cols = pl.ds(pl.multiple_of(k * C, C), C)
            cen[k] = (tok[:, cols].astype(F32) - dbias[:, cols]).astype(BF16)
            for w in range(2):
                hop(0, w, k).start()

        @pl.when(k == 0)
        def _():
            build_meta()
            for w in range(2):
                tgt_hop(0, w).start()
                meta_hop(0, w).start()
            own = placing(tgt[...], z, 0, NS)
            put(pown, tpown, 0, own)
            to_peers(ms, 0, pick_rows(own, meta[...]))
            enc_copy.wait()

        @pl.when((k >= 1) & (k <= F))
        def _():
            for w in range(2):
                hop(0, w, k - 1).wait_recv()
                hop(1, w, k - 1).start()

        @pl.when(k == 1)
        def _():
            for w in range(2):
                tgt_hop(0, w).wait_recv()
                meta_hop(0, w).wait_recv()
                tgt_hop(1, w).start()
                meta_hop(1, w).start()
                one = placing(tgt1[w], z, 0, NS)
                put(pone.at[w], tpone.at[w], 0, one)
                to_peers(ms, 1 + w, pick_rows(one, m1[w]))

        @pl.when(k == 2)
        def _():
            for w in range(2):
                step = 1 - 2 * w
                tgt_hop(1, w).wait_recv()
                meta_hop(1, w).wait_recv()
                near = placing(tgt2[w], z, 0, NS)
                put(ptwo.at[w], tptwo.at[w], 0, near)
                to_peers(ms, 3 + w, pick_rows(near, m2[w]))
                far = placing(tgt2[w], plane_of(step), 0, NS)
                put(ptwo.at[w], tptwo.at[w], NS, far)
                m3s[w, 0:NS, :] = pick_rows(far, m2[w])
                last = placing(tgt2[w], plane_of(2 * step), HALF * w, HALF)
                put(ptwo.at[w], tptwo.at[w], 2 * NS, last)
                m3s[w, NS:NS + HALF, :] = pick_rows(last, m2[w])
                meta_hop(2, w).start()

        @pl.when((k >= 2) & (k <= F + 1))
        def _():
            f = k - 2
            for w in range(2):
                hop(1, w, f).wait_recv()
                two = dot(ptwo[w], r2[w, f]).astype(BF16)
                s3[w, f] = two[NS:, :]
                hop(2, w, f).start()
                to_peers(xsa.at[f], 3 + w, two[0:NS, :])

        @pl.when((k >= 3) & (k <= F + 2))
        def _():
            f = k - 3
            for w in range(2):
                hop(2, w, f).wait_recv()
                hop(3, w, f).start()
                to_peers(xsb.at[f], w, r3[w, f, 0:NS, :])

        @pl.when(k == 3)
        def _():
            for w in range(2):
                meta_hop(2, w).wait_recv()
                meta_hop(3, w).start()
                to_peers(ms, 5 + w, m3[w, 0:NS, :])

        @pl.when((k >= 4) & (k <= F + 3))
        def _():
            f = k - 4
            for w in range(2):
                hop(3, w, f).wait_recv()
            to_peers(xsb.at[f], 2, jnp.concatenate([r4[0, f], r4[1, f]], axis=0))
            out_b(f).start()

        @pl.when(k == 4)
        def _():
            for w in range(2):
                meta_hop(3, w).wait_recv()
            to_peers(ms, 7, jnp.concatenate([m4[0], m4[1]], axis=0))
            meta_x.start()

        @pl.when((k >= 2) & (k <= F + 1))
        def _():
            f = k - 2
            to_peers(xsa.at[f], 0, dot(pown[...], cen[f]).astype(BF16))
            for w in range(2):
                to_peers(xsa.at[f], 1 + w, dot(pone[w], r1[w, f]).astype(BF16))
            out_a(f).start()

        @pl.when((k >= 3) & (k <= F + 2))
        def _():
            f = k - 3
            out_a(f).wait_recv()
            encode(acc_a, xra[f].reshape(NP * GA * CAP, C), f)

        @pl.when(k == 5)
        def _():
            meta_x.wait_recv()
            read_picks(0, GA, idx_a)
            read_picks(GA, GA + GB, idx_b)

        @pl.when(k == F + 3)
        def _():
            pick_values(acc_a, idx_a, act_a.shape[0] // 128, ya)
            for turn in range(1, Y):
                y_copy(turn, ya, yar, 0).start()
            dec_copy.wait()

        @pl.when(k == F + 4)
        def _():
            for turn in range(1, Y):
                y_copy(turn, ya, yar, 0).wait_recv()
            spread_values(ya, yar, idx_a, act_a.shape[0] // 128, act_a)

        @pl.when(k >= 5)
        def _():
            f = k - 5
            out_b(f).wait_recv()
            encode(acc_b, xrb[f].reshape(NP * GB * CAP, C), f)

    pick_values(acc_b, idx_b, act_b.shape[0] // 128, yb)
    for turn in range(1, Y):
        y_copy(turn, yb, ybr, 1).start()
    for turn in range(1, Y):
        y_copy(turn, yb, ybr, 1).wait_recv()
    spread_values(yb, ybr, idx_b, act_b.shape[0] // 128, act_b)

    def slots(ref, g):
        return ref[:, g * CAP:(g + 1) * CAP, :].reshape(NS, C)

    @pl.loop(0, F + 5)
    def _(k):
        @pl.when(k < F)
        def _():
            decode(act_b, ysb.at[k], k)
            home_b(k).start()

        @pl.when((k >= 5) & (k <= F + 4))
        def _():
            f = k - 5
            whole = dot(tpown[...], slots(yra.at[f], 0))
            for w in range(2):
                back(0, w, f).wait_recv()
                whole = whole + t1[w, f].astype(F32)
            cols = pl.ds(pl.multiple_of(f * C, C), C)
            out[:, cols] = (whole + dbias[:, cols]).astype(BF16)

        @pl.when((k >= 4) & (k <= F + 3))
        def _():
            f = k - 4
            for w in range(2):
                part = dot(tpone[w], slots(yra.at[f], 1 + w))
                back(1, w, f).wait_recv()
                b1[w, f] = (part + t2[w, f].astype(F32)).astype(BF16)
                back(0, w, f).start()

        @pl.when((k >= 3) & (k <= F + 2))
        def _():
            f = k - 3
            home_a(f).wait_recv()
            for w in range(2):
                part = dot(tptwo[w, :, 0:NS], slots(yra.at[f], 3 + w))
                back(2, w, f).wait_recv()
                part = part + dot(tptwo[w, :, NS:2 * NS], t3[w, f, 0:NS, :])
                part = part + dot(tptwo[w, :, 2 * NS:2 * NS + HALF], t3[w, f, NS:NS + HALF, :])
                b2[w, f] = part.astype(BF16)
                back(1, w, f).start()

        @pl.when((k >= 2) & (k <= F + 1))
        def _():
            f = k - 2
            for w in range(2):
                b3[w, f, 0:NS, :] = slots(yrb.at[f], w)
                back(3, w, f).wait_recv()
                b3[w, f, NS:NS + HALF, :] = t4[w, f]
                back(2, w, f).start()

        @pl.when((k >= 1) & (k <= F))
        def _():
            f = k - 1
            home_b(f).wait_recv()
            last = slots(yrb.at[f], 2)
            for w in range(2):
                b4[w, f] = last[HALF * w:HALF * (w + 1), :]
                back(3, w, f).start()
            decode(act_a, ysa.at[f], f)
            home_a(f).start()

        @pl.when(k < F)
        def _():
            for h in range(4):
                for w in range(2):
                    hop(h, w, k).wait_send()
            out_a(k).wait_send()
            out_b(k).wait_send()

        @pl.when(k >= 5)
        def _():
            for h in range(4):
                for w in range(2):
                    back(h, w, k - 5).wait_send()
            home_a(k - 5).wait_send()
            home_b(k - 5).wait_send()

    for w in range(2):
        for h in range(4):
            meta_hop(h, w).wait_send()
        for h in range(2):
            tgt_hop(h, w).wait_send()
    meta_x.wait_send()
    for turn in range(1, Y):
        y_copy(turn, ya, yar, 0).wait_send()
        y_copy(turn, yb, ybr, 1).wait_send()


def on_device(tokens, dec_bias, routes, latent_picks, enc_weight, dec_weight, enc_bias):
    rows, width = tokens.shape
    lat = enc_weight.shape[2]
    top = routes.shape[1]
    Y = lax.axis_size("dp")
    nblk = lax.axis_size("blocks")
    NP = nblk // RING
    NS = NP * CAP
    HALF = NS // 2
    F = CHUNKS
    C = width // F
    GA, GB = 5, 3
    na, nb = NP * GA * CAP, NP * GB * CAP
    V = pltpu.VMEM
    D = pltpu.SemaphoreType.DMA
    scratch = [
        V((width, lat), BF16), V((lat, width), BF16),
        V((F, rows, C), BF16), V((2, F, rows, C), BF16), V((2, F, rows, C), BF16),
        V((2, F, NS + HALF, C), BF16), V((2, F, NS + HALF, C), BF16), V((2, F, HALF, C), BF16),
        V((F, NP, GA * CAP, C), BF16), V((F, NP, GB * CAP, C), BF16),
        V((F, NP, GA * CAP, C), BF16), V((F, NP, GB * CAP, C), BF16),
        V((na, lat), F32), V((nb, lat), F32), V((na, lat), BF16), V((nb, lat), BF16),
        V((F, NP, GA * CAP, C), BF16), V((F, NP, GB * CAP, C), BF16),
        V((F, NP, GA * CAP, C), BF16), V((F, NP, GB * CAP, C), BF16),
        V((2, F, HALF, C), BF16), V((2, F, NS + HALF, C), BF16),
        V((2, F, rows, C), BF16), V((2, F, rows, C), BF16),
        V((2, F, HALF, C), BF16), V((2, F, NS + HALF, C), BF16),
        V((2, F, rows, C), BF16), V((2, F, rows, C), BF16),
        V((NS, rows), BF16), V((2, NS, rows), BF16), V((2, 2 * NS + HALF, rows), BF16),
        V((rows, NS), BF16), V((2, rows, NS), BF16), V((2, rows, 3 * NS), BF16),
        V((8, rows), F32), V((2, 8, rows), F32), V((2, 8, rows), F32),
        V((rows, 128), BF16), V((2, rows, 128), BF16), V((2, rows, 128), BF16),
        V((2, NS + HALF, 128), BF16), V((2, NS + HALF, 128), BF16), V((2, HALF, 128), BF16),
        V((NP, 8 * CAP, 128), BF16), V((NP, 8 * CAP, 128), BF16),
        V((na, 128), jnp.int32), V((nb, 128), jnp.int32),
        V((na // 128 * CAP, 128), F32), V((nb // 128 * CAP, 128), F32),
        V((max(Y - 1, 1), na // 128 * CAP, 128), F32), V((max(Y - 1, 1), nb // 128 * CAP, 128), F32),
        D((2,)), D((4, 2, F)), D((4, 2, F)), D((4, 2, F)), D((4, 2, F)),
        D((2, F)), D((2, F)), D((2, F)), D((2, F)), D((2, F)), D((2, F)),
        D((6, 2)), D((6, 2)), D((3,)), D((2, max(Y - 1, 1))), D((2, max(Y - 1, 1))),
    ]
    vmem = pl.BlockSpec(memory_space=pltpu.VMEM)
    hbm = pl.BlockSpec(memory_space=pl.ANY)
    return pl.pallas_call(
        kernel,
        out_shape=jax.ShapeDtypeStruct((rows, width), BF16),
        in_specs=[vmem] * 5 + [hbm] * 2,
        out_specs=vmem,
        scratch_shapes=scratch,
        compiler_params=pltpu.CompilerParams(
            collective_id=0, has_side_effects=True, vmem_limit_bytes=63 * 1024 * 1024
        ),
    )(
        tokens, dec_bias.reshape(1, width), routes, latent_picks.reshape(rows, -1), enc_bias,
        enc_weight, dec_weight,
    )


def solution(mesh):
    in_specs = (
        P("blocks", "dp"),
        P("dp"),
        P("blocks", None),
        P("blocks", None, None),
        P("blocks", "dp", None),
        P("blocks", None, "dp"),
        P("blocks", None),
    )
    return jax.shard_map(
        on_device, mesh=mesh, in_specs=in_specs, out_specs=P("blocks", "dp"), check_vma=False
    )
```

```python
import functools

import jax
import jax.numpy as jnp
from jax import lax
from jax.experimental import pallas as pl
from jax.experimental.pallas import tpu as pltpu
from jax.sharding import PartitionSpec as P

F32 = jnp.float32
BF16 = jnp.bfloat16
MESH = pl.DeviceIdType.MESH
RING = 8
CORES = 2
CAP = 16
CHUNKS = 16
HOP = 2
EARLY = 4
SWAP = 3
PARTS = 4
GROUPS = 8


def dot(a, b):
    return jnp.dot(a, b, preferred_element_type=F32)


def iota(shape, axis):
    return lax.broadcasted_iota(jnp.int32, shape, axis)


def kernel(
    tok, dbias, routes, picks, ebias, enc_hbm, dec_hbm, out,
    enc, dec, cen, r1, r2, s3, r3, r4, xs, xr, acc, act, ys, yr,
    b4, b3, b2, b1, t4, t3, t2, t1,
    pown, pone, ptwo, tpown, tpone, tptwo,
    tgt, tgt1, tgt2, meta, m1, m2, m3s, m3, m4, ms, mr, idx, yv, yg,
    wsem, hs, hq, us, uq, xs_sem, xq_sem, xl_sem, vs_sem, vq_sem, vl_sem,
    ms_sem, mq_sem, mx_sem, mr_sem, ysem_s, ysem_q,
):
    rows = tok.shape[0]
    F, _, C = cen.shape
    NP = xs.shape[1]
    NX = NP // CORES
    NS = NP * CAP
    HALF = NS // 2
    top = routes.shape[0]
    lat = enc.shape[1]
    Y = lax.axis_size("dp")

    y = lax.axis_index("dp")
    b = lax.axis_index("blocks")
    core = lax.rem(b, CORES)
    z = lax.rem(lax.div(b, CORES), RING)
    x = lax.div(b, CORES * RING)
    me = x * CORES + core

    def block_of(p, plane):
        return (lax.div(p, CORES) * RING + plane) * CORES + lax.rem(p, CORES)

    def plane_of(step):
        return lax.rem(z + step + RING, RING)

    ahead = (block_of(me, plane_of(1)), block_of(me, plane_of(-1)))
    beyond = (block_of(me, plane_of(2)), block_of(me, plane_of(-2)))

    def to_peer(turn):
        p = lax.rem(me + turn, NP)
        return p, (y, block_of(p, z))

    def z_copy(src, dst, ssem, rsem, way, far=False):
        return pltpu.make_async_remote_copy(
            src_ref=src, dst_ref=dst, send_sem=ssem, recv_sem=rsem,
            device_id=(y, (beyond if far else ahead)[way]), device_id_type=MESH,
        )

    barrier = pltpu.get_barrier_semaphore()
    for way in range(2):
        pl.semaphore_signal(barrier, inc=1, device_id=(y, ahead[way]), device_id_type=MESH)
        pl.semaphore_signal(barrier, inc=1, device_id=(y, beyond[way]), device_id_type=MESH)
    for turn in range(1, NP):
        pl.semaphore_signal(barrier, inc=1, device_id=to_peer(turn)[1], device_id_type=MESH)
    for turn in range(1, Y):
        pl.semaphore_signal(
            barrier, inc=1, device_id=(lax.rem(y + turn, Y), b), device_id_type=MESH
        )
    enc_copy = pltpu.make_async_copy(enc_hbm.at[0], enc, wsem.at[0])
    dec_copy = pltpu.make_async_copy(dec_hbm.at[0], dec, wsem.at[1])
    enc_copy.start()
    dec_copy.start()
    pl.semaphore_wait(barrier, 4 + NP - 1 + Y - 1)

    def hop(h, w, f):
        src, dst = (
            (cen.at[f], r1.at[w, f]),
            (r1.at[w, f], r2.at[w, f]),
            (s3.at[w, f, pl.ds(0, NS)], r3.at[w, f]),
            (s3.at[w, f, pl.ds(NS, HALF)], r4.at[w, f]),
        )[h]
        return z_copy(src, dst, hs.at[h, w, f], hq.at[h, w, f], w, h == 3)

    def half_cols(f):
        return pl.ds(pl.multiple_of(lax.rem(f, 2) * C, C), C)

    def part_of(f, g, p, n):
        return yr.at[lax.div(f, 2), pl.ds(p, n), pl.ds(g * CAP, CAP), half_cols(f)]

    def back(h, w, f):
        src, dst = (
            (b1.at[w, f], t1.at[w, f]),
            (b2.at[w, f], t2.at[w, f]),
            (b3.at[w, f], t3.at[w, f]),
            (b4.at[w, f], t4.at[w, f]),
        )[h]
        return z_copy(src, dst, us.at[h, w, f], uq.at[h, w, f], 1 - w, h == 3)

    def meta_hop(h, w):
        src, dst = (
            (meta, m1.at[w]),
            (m1.at[w], m2.at[w]),
            (m3s.at[w, pl.ds(0, NS)], m3.at[w]),
            (m3s.at[w, pl.ds(NS, HALF)], m4.at[w]),
        )[h]
        return z_copy(src, dst, ms_sem.at[h, w], mq_sem.at[h, w], w, h == 3)

    def tgt_hop(h, w):
        src, dst = ((tgt, tgt1.at[w]), (tgt1.at[w], tgt2.at[w]))[h]
        return z_copy(src, dst, ms_sem.at[4 + h, w], mq_sem.at[4 + h, w], w)

    class Outward:
        def __init__(self, send, landing, ssem, rsem, lsem):
            self.send, self.landing, self.sems = send, landing, (ssem, rsem, lsem)

        def local(self):
            return pltpu.make_async_copy(self.send.at[me], self.landing.at[x], self.sems[2])

        def start(self):
            for turn in range(1, NP):
                p, device = to_peer(turn)
                pltpu.make_async_remote_copy(
                    src_ref=self.send.at[p], dst_ref=self.landing.at[x],
                    send_sem=self.sems[0], recv_sem=self.sems[1],
                    device_id=device, device_id_type=MESH,
                ).start()
            self.local().start()

        def wait_send(self):
            pltpu.make_async_remote_copy(
                src_ref=self.send.at[pl.ds(0, NP - 1)], dst_ref=self.send.at[pl.ds(0, NP - 1)],
                send_sem=self.sems[0], recv_sem=self.sems[1],
                device_id=to_peer(1)[1], device_id_type=MESH,
            ).wait_send()

        def wait_recv(self, stream):
            def pieces(n):
                pltpu.make_async_remote_copy(
                    src_ref=self.landing.at[pl.ds(0, n)], dst_ref=self.landing.at[pl.ds(0, n)],
                    send_sem=self.sems[0], recv_sem=self.sems[1],
                    device_id=to_peer(1)[1], device_id_type=MESH,
                ).wait_recv()

            @pl.when(stream == core)
            def _():
                if NX > 1:
                    pieces(NX - 1)
                self.local().wait()

            @pl.when(stream != core)
            def _():
                pieces(NX)

    def outward(g):
        f = lax.rem(g, F // 2)
        return Outward(xs.at[f], xr.at[g], xs_sem.at[f], xq_sem.at[g], xl_sem.at[f])

    def outward_meta(stream):
        return Outward(ms, mr.at[stream], mx_sem.at[0], mr_sem.at[stream], mx_sem.at[1])

    def homeward(g, turn):
        f, stream = lax.rem(g, F // 2), lax.div(g, F // 2)
        to = lax.rem(x + turn, NX)
        p = to * CORES + stream
        return pltpu.make_async_remote_copy(
            src_ref=ys.at[g, to], dst_ref=yr.at[f, me],
            send_sem=vs_sem.at[g], recv_sem=vq_sem.at[f],
            device_id=(y, block_of(p, z)), device_id_type=MESH,
        )

    def homeward_local(g):
        f = lax.rem(g, F // 2)
        return pltpu.make_async_copy(ys.at[g, x], yr.at[f, me], vl_sem.at[f])

    def homeward_start(g):
        stream = lax.div(g, F // 2)
        for turn in range(1, NX):
            homeward(g, turn).start()

        @pl.when(stream == core)
        def _():
            homeward_local(g).start()

        @pl.when(stream != core)
        def _():
            homeward(g, 0).start()

    def homeward_wait_send(g):
        def pieces(n):
            pltpu.make_async_remote_copy(
                src_ref=ys.at[g, pl.ds(0, n)], dst_ref=ys.at[g, pl.ds(0, n)],
                send_sem=vs_sem.at[g], recv_sem=vq_sem.at[0],
                device_id=to_peer(1)[1], device_id_type=MESH,
            ).wait_send()

        @pl.when(lax.div(g, F // 2) == core)
        def _():
            if NX > 1:
                pieces(NX - 1)

        @pl.when(lax.div(g, F // 2) != core)
        def _():
            pieces(NX)

    def homeward_wait_recv(f):
        pltpu.make_async_remote_copy(
            src_ref=yr.at[f, pl.ds(0, NP - 1)], dst_ref=yr.at[f, pl.ds(0, NP - 1)],
            send_sem=vs_sem.at[0], recv_sem=vq_sem.at[f],
            device_id=to_peer(1)[1], device_id_type=MESH,
        ).wait_recv()
        homeward_local(core * (F // 2) + f).wait()

    part_rows = acc.shape[1] // PARTS
    part_vals = part_rows // 128 * CAP

    def y_copy(turn, stream, half):
        at = pl.ds(half * part_vals, part_vals)
        return pltpu.make_async_remote_copy(
            src_ref=yv.at[stream, at], dst_ref=yg.at[stream, turn - 1, at],
            send_sem=ysem_s.at[stream, half, turn - 1], recv_sem=ysem_q.at[stream, half, turn - 1],
            device_id=(lax.rem(y + turn, Y), b), device_id_type=MESH,
        )

    def placing(targets, plane, first, count):
        q = iota((count, rows), 0) + first
        ids = ((lax.shift_right_logical(q, 5) * RING + plane) * CORES
               + (lax.shift_right_logical(q, 4) & 1)) * CAP + (q & (CAP - 1))
        ids = ids.astype(F32)
        return [jnp.where(targets[k:k + 1, :] == ids, 1.0, 0.0) for k in range(top)]

    def put(p_ref, t_ref, lo, kinds):
        whole = kinds[0]
        for other in kinds[1:]:
            whole = whole + other
        n = whole.shape[0]
        p_ref[lo:lo + n, :] = whole.astype(BF16)
        t_ref[:, lo:lo + n] = whole.T.astype(BF16)

    def pick_rows(kinds, source):
        total = None
        for k, one in enumerate(kinds):
            part = dot(one.astype(BF16), source).astype(BF16)
            take = (iota((128, 128), 0) == iota((128, 128), 1) + 32 * k) & (iota((128, 128), 1) < 32)
            part = dot(part, jnp.where(take, 1.0, 0.0).astype(BF16))
            total = part if total is None else total + part
        return total.astype(BF16)

    def to_pair(f, g, value):
        to_peers(xs.at[lax.div(f, 2), :, :, half_cols(f)], g, value)

    def to_peers(ref, g, value):
        ref[:, g * CAP:(g + 1) * CAP, :] = value.reshape(NP, CAP, value.shape[-1])

    def build_meta():
        tgt[...] = jnp.zeros(tgt.shape, F32)
        before = jnp.where(iota((rows, rows), 0) < iota((rows, rows), 1), 1.0, 0.0).astype(BF16)
        so_far = jnp.zeros((128, 1), F32)
        for k in range(top):
            owner = routes[k:k + 1, :]
            named = jnp.where(owner == iota((128, rows), 0), 1.0, 0.0)
            rank = jnp.sum(named * (dot(named.astype(BF16), before) + so_far), axis=0, keepdims=True)
            so_far = so_far + jnp.sum(named, axis=1, keepdims=True)
            tgt[k:k + 1, :] = owner.astype(F32) * CAP + rank
        chosen = picks[...]
        n = chosen.shape[0]
        lane, col = iota((128, n), 0), iota((128, n), 1)
        base = lax.shift_right_logical(col, 4) * 32 + (col & 15)
        hi = lax.shift_right_logical(chosen, 3).astype(F32).astype(BF16)
        lo = (chosen & 7).astype(F32).astype(BF16)
        meta[...] = (
            dot(jnp.where(lane == base, 1.0, 0.0).astype(BF16), hi)
            + dot(jnp.where(lane == base + 16, 1.0, 0.0).astype(BF16), lo)
        ).T.astype(BF16)

    def pick_values(stream, half):
        @pl.loop(0, part_rows // 128)
        def _(i):
            j = half * (part_rows // 128) + i
            at = pl.ds(pl.multiple_of(j * 128, 128), 128)
            ids = idx[stream, at, :]
            got = jnp.zeros((128, 128), F32)
            for tile in range(lat // 128):
                here = jnp.take_along_axis(
                    acc[stream, at, tile * 128:(tile + 1) * 128], ids & 127, axis=1,
                    mode="promise_in_bounds",
                )
                got = jnp.where(lax.shift_right_logical(ids, 7) == tile, here, got)
            yv[stream, pl.ds(pl.multiple_of(j * CAP, CAP), CAP), :] = got.T[0:CAP, :]

    def spread_values(stream, half):
        @pl.loop(0, part_rows // 128)
        def _(i):
            j = half * (part_rows // 128) + i
            small = pl.ds(pl.multiple_of(j * CAP, CAP), CAP)
            value = yv[stream, small, :]
            for turn in range(1, Y):
                value = value + yg[stream, turn - 1, small, :]
            value = jnp.maximum(value, 0.0)
            value = jnp.concatenate([value, jnp.zeros((128 - CAP, 128), F32)], axis=0).T
            ids = idx[stream, pl.ds(pl.multiple_of(j * 128, 128), 128), :]
            lane = iota((32, lat), 1)
            for part in range(4):
                sub = slice(part * 32, (part + 1) * 32)
                full = jnp.zeros((32, lat), F32)
                for i in range(CAP):
                    full = jnp.where(lane == ids[sub, i:i + 1], value[sub, i:i + 1], full)
                at = pl.ds(pl.multiple_of(j * 128 + part * 32, 32), 32)
                act[stream, at, :] = full.astype(BF16)

    def read_picks(stream):
        one = mr[stream].reshape(acc.shape[1], 128)
        j, i = iota((128, 128), 0), iota((128, 128), 1)
        weigh = jnp.where(j == i, 8.0, jnp.where(j == i + 16, 1.0, 0.0))
        weigh = jnp.where(i < 16, weigh, 0.0).astype(BF16)
        idx[stream] = dot(one, weigh).astype(jnp.int32)

    def encode(g):
        f, stream = lax.rem(g, F // 2), lax.div(g, F // 2)
        value = xr[g].reshape(acc.shape[1], 2 * C)
        at = pl.ds(pl.multiple_of(f * 2 * C, 2 * C), 2 * C)
        width = min(lat, 256)

        @pl.loop(0, lat // width)
        def _(n):
            cols = pl.ds(pl.multiple_of(n * width, width), width)
            acc[stream, :, cols] += dot(value, enc[at, cols])

    def decode(g):
        f, stream = lax.rem(g, F // 2), lax.div(g, F // 2)
        at = pl.ds(pl.multiple_of(f * 2 * C, 2 * C), 2 * C)
        ys[g] = dot(act[stream], dec[:, at]).astype(BF16).reshape(NX, NS, 2 * C)

    def slots(f, g):
        return part_of(f, g, 0, NP)[...].reshape(NS, C)

    def within(n, count):
        return (n >= 0) & (n < count)

    encoding = 3 * HOP + SWAP
    home = max(2 * F - EARLY, F + encoding + PARTS + 1)
    ending = SWAP + 3 * HOP

    @pl.loop(0, home + 2 * F + ending + 2)
    def _(k):
        own = k - core * F

        @pl.when(within(own, F))
        def _():
            cols = pl.ds(pl.multiple_of(own * C, C), C)
            cen[own] = (tok[:, cols].astype(F32) - dbias[:, cols]).astype(BF16)
            for w in range(2):
                hop(0, w, own).start()

        @pl.when(k == 0)
        def _():
            bias = ebias[...] * jnp.where(y == 0, 1.0, 0.0)
            for stream in range(CORES):
                acc[stream] = jnp.broadcast_to(bias, acc.shape[1:])

        @pl.when(own == 0)
        def _():
            build_meta()
            for w in range(2):
                tgt_hop(0, w).start()
                meta_hop(0, w).start()
            kinds = placing(tgt[...], z, 0, NS)
            put(pown, tpown, 0, kinds)
            to_peers(ms, 0, pick_rows(kinds, meta[...]))

        @pl.when(within(own - HOP, F))
        def _():
            for w in range(2):
                hop(0, w, own - HOP).wait_recv()
                hop(1, w, own - HOP).start()

        @pl.when(own == HOP)
        def _():
            for w in range(2):
                tgt_hop(0, w).wait_recv()
                meta_hop(0, w).wait_recv()
                tgt_hop(1, w).start()
                meta_hop(1, w).start()
                kinds = placing(tgt1[w], z, 0, NS)
                put(pone.at[w], tpone.at[w], 0, kinds)
                to_peers(ms, 1 + w, pick_rows(kinds, m1[w]))

        @pl.when(own == 2 * HOP)
        def _():
            for w in range(2):
                step = 1 - 2 * w
                tgt_hop(1, w).wait_recv()
                meta_hop(1, w).wait_recv()
                near = placing(tgt2[w], z, 0, NS)
                put(ptwo.at[w], tptwo.at[w], 0, near)
                to_peers(ms, 3 + w, pick_rows(near, m2[w]))
                far = placing(tgt2[w], plane_of(step), 0, NS)
                put(ptwo.at[w], tptwo.at[w], NS, far)
                m3s[w, 0:NS, :] = pick_rows(far, m2[w])
                last = placing(tgt2[w], plane_of(2 * step), HALF * w, HALF)
                put(ptwo.at[w], tptwo.at[w], 2 * NS, last)
                m3s[w, NS:NS + HALF, :] = pick_rows(last, m2[w])
                meta_hop(2, w).start()
                meta_hop(3, w).start()

        @pl.when(within(own - 2 * HOP, F))
        def _():
            f = own - 2 * HOP
            for w in range(2):
                hop(1, w, f).wait_recv()
                two = dot(ptwo[w], r2[w, f]).astype(BF16)
                s3[w, f] = two[NS:, :]
                hop(2, w, f).start()
                hop(3, w, f).start()
                to_pair(f, 3 + w, two[0:NS, :])

        @pl.when(within(own - 3 * HOP, F))
        def _():
            f = own - 3 * HOP
            for w in range(2):
                hop(2, w, f).wait_recv()
                hop(3, w, f).wait_recv()
                to_pair(f, 5 + w, r3[w, f])
            to_pair(f, 7, jnp.concatenate([r4[0, f], r4[1, f]], axis=0))

            @pl.when(lax.rem(f, 2) == 1)
            def _():
                outward(core * (F // 2) + lax.div(f, 2)).start()

        @pl.when(own == 3 * HOP)
        def _():
            for w in range(2):
                meta_hop(2, w).wait_recv()
                meta_hop(3, w).wait_recv()
                to_peers(ms, 5 + w, m3[w])
            to_peers(ms, 7, jnp.concatenate([m4[0], m4[1]], axis=0))
            outward_meta(core).start()

        @pl.when(within(own - 2 * HOP, F))
        def _():
            f = own - 2 * HOP
            to_pair(f, 0, dot(pown[...], cen[f]).astype(BF16))
            for w in range(2):
                to_pair(f, 1 + w, dot(pone[w], r1[w, f]).astype(BF16))

        done = k - home - core * F

        @pl.when(within(done - SWAP - 2 * HOP, F))
        def _():
            f = done - SWAP - 2 * HOP
            for w in range(2):
                part = dot(tpone[w], slots(f, 1 + w))
                back(1, w, f).wait_recv()
                b1[w, f] = (part + t2[w, f].astype(F32)).astype(BF16)
                back(0, w, f).start()

        @pl.when(within(done - SWAP - HOP, F))
        def _():
            f = done - SWAP - HOP
            for w in range(2):
                part = dot(tptwo[w, :, 0:NS], slots(f, 3 + w))
                back(2, w, f).wait_recv()
                part = part + dot(tptwo[w, :, NS:2 * NS], t3[w, f])
                back(3, w, f).wait_recv()
                part = part + dot(tptwo[w, :, 2 * NS:2 * NS + HALF], t4[w, f])
                b2[w, f] = part.astype(BF16)
                back(1, w, f).start()

        @pl.when(within(done - SWAP, F))
        def _():
            f = done - SWAP

            @pl.when(lax.rem(f, 2) == 0)
            def _():
                homeward_wait_recv(lax.div(f, 2))
            last = slots(f, 7)
            for w in range(2):
                b4[w, f] = last[HALF * w:HALF * (w + 1), :]
                back(3, w, f).start()
                b3[w, f] = slots(f, 5 + w)
                back(2, w, f).start()

        @pl.when(k == 3 * HOP)
        def _():
            enc_copy.wait()
            dec_copy.wait()

        @pl.when(within(k - encoding, 2 * F) & (lax.rem(k - encoding, 2) == 1))
        def _():
            g = lax.div(k - encoding, 2)
            outward(g).wait_recv(lax.div(g, F // 2))
            encode(g)

        for stream in range(CORES):
            @pl.when(k == stream * F + encoding)
            def _():
                outward_meta(stream).wait_recv(stream)
                read_picks(stream)

        second = jnp.where(k >= 2 * F + encoding, 1, 0)
        turn_step = k - (F + encoding) - second * F

        @pl.when(within(turn_step, PARTS))
        def _():
            pick_values(second, turn_step)
            for turn in range(1, Y):
                y_copy(turn, second, turn_step).start()

        @pl.when(within(turn_step - 2, PARTS))
        def _():
            for turn in range(1, Y):
                y_copy(turn, second, turn_step - 2).wait_recv()
            spread_values(second, turn_step - 2)

        @pl.when(within(k - home, 2 * F) & (lax.rem(k - home, 2) == 0))
        def _():
            g = lax.div(k - home, 2)
            decode(g)
            homeward_start(g)

        @pl.when(within(done - ending, F))
        def _():
            f = done - ending
            whole = dot(tpown[...], slots(f, 0))
            for w in range(2):
                back(0, w, f).wait_recv()
                whole = whole + t1[w, f].astype(F32)
            cols = pl.ds(pl.multiple_of(f * C, C), C)
            out[:, cols] = (whole + dbias[:, cols]).astype(BF16)

        @pl.when(within(k - home - 3, F))
        def _():
            f = k - home - 3
            for h in range(4):
                for w in range(2):
                    hop(h, w, f).wait_send()

            @pl.when(lax.rem(f, 2) == 1)
            def _():
                outward(core * (F // 2) + lax.div(f, 2)).wait_send()

        @pl.when(within(done - ending - 1, F))
        def _():
            for h in range(4):
                for w in range(2):
                    back(h, w, done - ending - 1).wait_send()

        @pl.when(within(k - home - SWAP - 4, 2 * F) & (lax.rem(k - home - SWAP - 4, 2) == 0))
        def _():
            homeward_wait_send(lax.div(k - home - SWAP - 4, 2))

    for w in range(2):
        for h in range(4):
            meta_hop(h, w).wait_send()
        for h in range(2):
            tgt_hop(h, w).wait_send()
    outward_meta(core).wait_send()
    for stream in range(CORES):
        for half in range(PARTS):
            for turn in range(1, Y):
                y_copy(turn, stream, half).wait_send()


def on_device(tokens, dec_bias, routes, latent_picks, enc_weight, dec_weight, enc_bias):
    rows, width = tokens.shape
    lat = enc_weight.shape[2]
    Y = lax.axis_size("dp")
    nblk = lax.axis_size("blocks")
    NP = nblk // RING
    NX = NP // CORES
    NS = NP * CAP
    HALF = NS // 2
    F = CHUNKS
    C = width // F
    piece = GROUPS * CAP
    n = NX * piece
    vals = n // 128 * CAP
    V = pltpu.VMEM
    D = pltpu.SemaphoreType.DMA
    scratch = [
        V((width, lat), BF16), V((lat, width), BF16),
        V((F, rows, C), BF16), V((2, F, rows, C), BF16), V((2, F, rows, C), BF16),
        V((2, F, NS + HALF, C), BF16), V((2, F, NS, C), BF16), V((2, F, HALF, C), BF16),
        V((F // 2, NP, piece, 2 * C), BF16), V((CORES * (F // 2), NX, piece, 2 * C), BF16),
        V((CORES, n, lat), F32), V((CORES, n, lat), BF16),
        V((CORES * (F // 2), NX, piece, 2 * C), BF16), V((F // 2, NP, piece, 2 * C), BF16),
        V((2, F, HALF, C), BF16), V((2, F, NS, C), BF16),
        V((2, F, rows, C), BF16), V((2, F, rows, C), BF16),
        V((2, F, HALF, C), BF16), V((2, F, NS, C), BF16),
        V((2, F, rows, C), BF16), V((2, F, rows, C), BF16),
        V((NS, rows), BF16), V((2, NS, rows), BF16), V((2, 2 * NS + HALF, rows), BF16),
        V((rows, NS), BF16), V((2, rows, NS), BF16), V((2, rows, 3 * NS), BF16),
        V((8, rows), F32), V((2, 8, rows), F32), V((2, 8, rows), F32),
        V((rows, 128), BF16), V((2, rows, 128), BF16), V((2, rows, 128), BF16),
        V((2, NS + HALF, 128), BF16), V((2, NS, 128), BF16), V((2, HALF, 128), BF16),
        V((NP, piece, 128), BF16), V((CORES, NX, piece, 128), BF16),
        V((CORES, n, 128), jnp.int32), V((CORES, vals, 128), F32),
        V((CORES, max(Y - 1, 1), vals, 128), F32),
        D((2,)), D((4, 2, F)), D((4, 2, F)), D((4, 2, F)), D((4, 2, F)),
        D((F // 2,)), D((F,)), D((F // 2,)), D((F,)), D((F // 2,)), D((F // 2,)),
        D((6, 2)), D((6, 2)), D((2,)), D((CORES,)),
        D((CORES, PARTS, max(Y - 1, 1))), D((CORES, PARTS, max(Y - 1, 1))),
    ]
    vmem = pl.BlockSpec(memory_space=pltpu.VMEM)
    hbm = pl.BlockSpec(memory_space=pl.ANY)
    return pl.pallas_call(
        kernel,
        out_shape=jax.ShapeDtypeStruct((rows, width), BF16),
        in_specs=[vmem] * 5 + [hbm] * 2,
        out_specs=vmem,
        scratch_shapes=scratch,
        compiler_params=pltpu.CompilerParams(
            collective_id=0, has_side_effects=True, vmem_limit_bytes=63 * 1024 * 1024
        ),
    )(
        tokens, dec_bias.reshape(1, width), routes.T,
        latent_picks.transpose(1, 2, 0).reshape(-1, rows), enc_bias, enc_weight, dec_weight,
    )


def solution(mesh):
    in_specs = (
        P("blocks", "dp"),
        P("dp"),
        P("blocks", None),
        P("blocks", None, None),
        P("blocks", "dp", None),
        P("blocks", None, "dp"),
        P("blocks", None),
    )
    return jax.shard_map(
        on_device, mesh=mesh, in_specs=in_specs, out_specs=P("blocks", "dp"), check_vma=False
    )
```

```python
import functools

import jax
import jax.numpy as jnp
from jax import lax
from jax.experimental import pallas as pl
from jax.experimental.pallas import tpu as pltpu
from jax.sharding import PartitionSpec as P

F32 = jnp.float32
BF16 = jnp.bfloat16
MESH = pl.DeviceIdType.MESH
RING = 8
CORES = 2
CAP = 16
CHUNKS = 16
HOP = 3
LEAD = 2
GAP = 0
EARLY = 4
SWAP = 3
PARTS = 2
GROUPS = 8


def dot(a, b):
    return jnp.dot(a, b, preferred_element_type=F32)


def iota(shape, axis):
    return lax.broadcasted_iota(jnp.int32, shape, axis)


def kernel(
    tok, dbias, routes, picks, ebias, enc_hbm, dec_hbm, out,
    enc, dec, cen, r1, r2, s3, r3, r4, xs, xr, acc, act, ys, yr,
    b4, b3, b2, b1, t4, t3, t2, t1,
    pown, pone, ptwo, tpown, tpone, tptwo,
    tgt, tgt1, tgt2, meta, m1, m2, m3s, m3, m4, ms, mr, idx, yv, yg,
    wsem, hs, hq, us, uq, xs_sem, xq_sem, xl_sem, vs_sem, vq_sem, vl_sem,
    ms_sem, mq_sem, mx_sem, mr_sem, ysem_s, ysem_q,
):
    rows = tok.shape[0]
    F, _, C = cen.shape
    NP = xs.shape[1]
    NX = NP // CORES
    NS = NP * CAP
    HALF = NS // 2
    top = routes.shape[0]
    lat = enc.shape[1]
    Y = lax.axis_size("dp")

    y = lax.axis_index("dp")
    b = lax.axis_index("blocks")
    core = lax.rem(b, CORES)
    z = lax.rem(lax.div(b, CORES), RING)
    x = lax.div(b, CORES * RING)
    me = x * CORES + core

    def block_of(p, plane):
        return (lax.div(p, CORES) * RING + plane) * CORES + lax.rem(p, CORES)

    def plane_of(step):
        return lax.rem(z + step + RING, RING)

    ahead = (block_of(me, plane_of(1)), block_of(me, plane_of(-1)))
    beyond = (block_of(me, plane_of(2)), block_of(me, plane_of(-2)))

    def to_peer(turn):
        p = lax.rem(me + turn, NP)
        return p, (y, block_of(p, z))

    def z_copy(src, dst, ssem, rsem, way, far=False):
        return pltpu.make_async_remote_copy(
            src_ref=src, dst_ref=dst, send_sem=ssem, recv_sem=rsem,
            device_id=(y, (beyond if far else ahead)[way]), device_id_type=MESH,
        )

    barrier = pltpu.get_barrier_semaphore()
    for way in range(2):
        pl.semaphore_signal(barrier, inc=1, device_id=(y, ahead[way]), device_id_type=MESH)
        pl.semaphore_signal(barrier, inc=1, device_id=(y, beyond[way]), device_id_type=MESH)
    for turn in range(1, NP):
        pl.semaphore_signal(barrier, inc=1, device_id=to_peer(turn)[1], device_id_type=MESH)
    for turn in range(1, Y):
        pl.semaphore_signal(
            barrier, inc=1, device_id=(lax.rem(y + turn, Y), b), device_id_type=MESH
        )
    enc_copy = pltpu.make_async_copy(enc_hbm.at[0], enc, wsem.at[0])
    dec_copy = pltpu.make_async_copy(dec_hbm.at[0], dec, wsem.at[1])
    enc_copy.start()
    dec_copy.start()
    pl.semaphore_wait(barrier, 4 + NP - 1 + Y - 1)

    def hop(h, w, f):
        src, dst = (
            (cen.at[f], r1.at[f, w]),
            (r1.at[f, w], r2.at[f, w]),
            (s3.at[w, f, pl.ds(0, NS)], r3.at[f, w]),
            (s3.at[w, f, pl.ds(NS, HALF)], r4.at[f, w]),
        )[h]
        return z_copy(src, dst, hs.at[h, w], hq.at[h, f], w, h == 3)

    def landed(ref, sem):
        pltpu.make_async_remote_copy(
            src_ref=ref, dst_ref=ref, send_sem=mq_sem.at[0, 0], recv_sem=sem,
            device_id=to_peer(1)[1], device_id_type=MESH,
        ).wait_recv()

    def hop_landed(h, f):
        landed((r1, r2, r3, r4)[h].at[f], hq.at[h, f])

    def back_landed(h, f):
        landed((t1, t2, t3, t4)[h].at[f], uq.at[h, f])

    def half_cols(f):
        return pl.ds(pl.multiple_of(lax.rem(f, 2) * C, C), C)

    def part_of(f, g, p, n):
        return yr.at[lax.div(f, 2), pl.ds(p, n), pl.ds(g * CAP, CAP), half_cols(f)]

    def back(h, w, f):
        src, dst = (
            (b1.at[w, f], t1.at[f, w]),
            (b2.at[w, f], t2.at[f, w]),
            (b3.at[w, f], t3.at[f, w]),
            (b4.at[w, f], t4.at[f, w]),
        )[h]
        return z_copy(src, dst, us.at[h, w], uq.at[h, f], 1 - w, h == 3)

    def meta_hop(h, w):
        src, dst = (
            (meta, m1.at[w]),
            (m1.at[w], m2.at[w]),
            (m3s.at[w, pl.ds(0, NS)], m3.at[w]),
            (m3s.at[w, pl.ds(NS, HALF)], m4.at[w]),
        )[h]
        return z_copy(src, dst, ms_sem.at[h, w], mq_sem.at[h, w], w, h == 3)

    def tgt_hop(h, w):
        src, dst = ((tgt, tgt1.at[w]), (tgt1.at[w], tgt2.at[w]))[h]
        return z_copy(src, dst, ms_sem.at[4 + h, w], mq_sem.at[4 + h, w], w)

    class Outward:
        def __init__(self, send, landing, ssem, rsem, lsem):
            self.send, self.landing, self.sems = send, landing, (ssem, rsem, lsem)

        def local(self):
            return pltpu.make_async_copy(self.send.at[me], self.landing.at[x], self.sems[2])

        def start(self):
            for turn in range(1, NP):
                p, device = to_peer(turn)
                pltpu.make_async_remote_copy(
                    src_ref=self.send.at[p], dst_ref=self.landing.at[x],
                    send_sem=self.sems[0], recv_sem=self.sems[1],
                    device_id=device, device_id_type=MESH,
                ).start()
            self.local().start()

        def wait_recv(self, stream):
            def pieces(n):
                pltpu.make_async_remote_copy(
                    src_ref=self.landing.at[pl.ds(0, n)], dst_ref=self.landing.at[pl.ds(0, n)],
                    send_sem=self.sems[0], recv_sem=self.sems[1],
                    device_id=to_peer(1)[1], device_id_type=MESH,
                ).wait_recv()

            @pl.when(stream == core)
            def _():
                if NX > 1:
                    pieces(NX - 1)
                self.local().wait()

            @pl.when(stream != core)
            def _():
                pieces(NX)

    def outward(g):
        f = lax.rem(g, F // 2)
        return Outward(xs.at[f], xr.at[g], xs_sem.at[0], xq_sem.at[g], xl_sem.at[f])

    def outward_meta(stream):
        return Outward(ms, mr.at[stream], mx_sem.at[0], mr_sem.at[stream], mx_sem.at[1])

    def homeward(g, turn):
        f, stream = lax.rem(g, F // 2), lax.div(g, F // 2)
        to = lax.rem(x + turn, NX)
        p = to * CORES + stream
        return pltpu.make_async_remote_copy(
            src_ref=ys.at[g, to], dst_ref=yr.at[f, me],
            send_sem=vs_sem.at[0], recv_sem=vq_sem.at[f],
            device_id=(y, block_of(p, z)), device_id_type=MESH,
        )

    def homeward_local(g):
        f = lax.rem(g, F // 2)
        return pltpu.make_async_copy(ys.at[g, x], yr.at[f, me], vl_sem.at[f])

    def homeward_start(g):
        stream = lax.div(g, F // 2)
        for turn in range(1, NX):
            homeward(g, turn).start()

        @pl.when(stream == core)
        def _():
            homeward_local(g).start()

        @pl.when(stream != core)
        def _():
            homeward(g, 0).start()

    def homeward_wait_recv(f):
        pltpu.make_async_remote_copy(
            src_ref=yr.at[f, pl.ds(0, NP - 1)], dst_ref=yr.at[f, pl.ds(0, NP - 1)],
            send_sem=vs_sem.at[0], recv_sem=vq_sem.at[f],
            device_id=to_peer(1)[1], device_id_type=MESH,
        ).wait_recv()
        homeward_local(core * (F // 2) + f).wait()

    part_rows = acc.shape[1] // PARTS
    part_vals = part_rows // 128 * CAP

    def y_copy(turn, stream, half):
        at = pl.ds(half * part_vals, part_vals)
        return pltpu.make_async_remote_copy(
            src_ref=yv.at[stream, at], dst_ref=yg.at[stream, turn - 1, at],
            send_sem=ysem_s.at[stream, half, turn - 1], recv_sem=ysem_q.at[stream, half, turn - 1],
            device_id=(lax.rem(y + turn, Y), b), device_id_type=MESH,
        )

    def placing(targets, plane, first, count):
        q = iota((count, rows), 0) + first
        ids = ((lax.shift_right_logical(q, 5) * RING + plane) * CORES
               + (lax.shift_right_logical(q, 4) & 1)) * CAP + (q & (CAP - 1))
        ids = ids.astype(F32)
        return [jnp.where(targets[k:k + 1, :] == ids, 1.0, 0.0) for k in range(top)]

    def put(p_ref, t_ref, lo, kinds):
        whole = kinds[0]
        for other in kinds[1:]:
            whole = whole + other
        n = whole.shape[0]
        p_ref[lo:lo + n, :] = whole.astype(BF16)
        t_ref[:, lo:lo + n] = whole.T.astype(BF16)

    def pick_rows(kinds, source):
        total = None
        for k, one in enumerate(kinds):
            part = dot(one.astype(BF16), source).astype(BF16)
            take = (iota((128, 128), 0) == iota((128, 128), 1) + 32 * k) & (iota((128, 128), 1) < 32)
            part = dot(part, jnp.where(take, 1.0, 0.0).astype(BF16))
            total = part if total is None else total + part
        return total.astype(BF16)

    def to_pair(f, g, value):
        to_peers(xs.at[lax.div(f, 2), :, :, half_cols(f)], g, value)

    def to_peers(ref, g, value):
        ref[:, g * CAP:(g + 1) * CAP, :] = value.reshape(NP, CAP, value.shape[-1])

    def build_meta():
        tgt[...] = jnp.zeros(tgt.shape, F32)
        before = jnp.where(iota((rows, rows), 0) < iota((rows, rows), 1), 1.0, 0.0).astype(BF16)
        so_far = jnp.zeros((128, 1), F32)
        for k in range(top):
            owner = routes[k:k + 1, :]
            named = jnp.where(owner == iota((128, rows), 0), 1.0, 0.0)
            rank = jnp.sum(named * (dot(named.astype(BF16), before) + so_far), axis=0, keepdims=True)
            so_far = so_far + jnp.sum(named, axis=1, keepdims=True)
            tgt[k:k + 1, :] = owner.astype(F32) * CAP + rank
        chosen = picks[...]
        n = chosen.shape[0]
        lane, col = iota((128, n), 0), iota((128, n), 1)
        base = lax.shift_right_logical(col, 4) * 32 + (col & 15)
        hi = lax.shift_right_logical(chosen, 3).astype(F32).astype(BF16)
        lo = (chosen & 7).astype(F32).astype(BF16)
        meta[...] = (
            dot(jnp.where(lane == base, 1.0, 0.0).astype(BF16), hi)
            + dot(jnp.where(lane == base + 16, 1.0, 0.0).astype(BF16), lo)
        ).T.astype(BF16)

    def pick_values(stream, half):
        @pl.loop(0, part_rows // 128)
        def _(i):
            j = half * (part_rows // 128) + i
            at = pl.ds(pl.multiple_of(j * 128, 128), 128)
            ids = idx[stream, at, :]
            got = jnp.zeros((128, 128), F32)
            for tile in range(lat // 128):
                here = jnp.take_along_axis(
                    acc[stream, at, tile * 128:(tile + 1) * 128], ids & 127, axis=1,
                    mode="promise_in_bounds",
                )
                got = jnp.where(lax.shift_right_logical(ids, 7) == tile, here, got)
            yv[stream, pl.ds(pl.multiple_of(j * CAP, CAP), CAP), :] = got.T[0:CAP, :]

    def spread_values(stream, half):
        @pl.loop(0, part_rows // 128)
        def _(i):
            j = half * (part_rows // 128) + i
            small = pl.ds(pl.multiple_of(j * CAP, CAP), CAP)
            value = yv[stream, small, :]
            for turn in range(1, Y):
                value = value + yg[stream, turn - 1, small, :]
            value = jnp.maximum(value, 0.0)
            value = jnp.concatenate([value, jnp.zeros((128 - CAP, 128), F32)], axis=0).T
            ids = idx[stream, pl.ds(pl.multiple_of(j * 128, 128), 128), :]
            lane = iota((32, lat), 1)
            for part in range(4):
                sub = slice(part * 32, (part + 1) * 32)
                full = jnp.zeros((32, lat), F32)
                for i in range(CAP):
                    full = jnp.where(lane == ids[sub, i:i + 1], value[sub, i:i + 1], full)
                at = pl.ds(pl.multiple_of(j * 128 + part * 32, 32), 32)
                act[stream, at, :] = full.astype(BF16)

    def read_picks(stream):
        one = mr[stream].reshape(acc.shape[1], 128)
        j, i = iota((128, 128), 0), iota((128, 128), 1)
        weigh = jnp.where(j == i, 8.0, jnp.where(j == i + 16, 1.0, 0.0))
        weigh = jnp.where(i < 16, weigh, 0.0).astype(BF16)
        idx[stream] = dot(one, weigh).astype(jnp.int32)

    def encode(g):
        f, stream = lax.rem(g, F // 2), lax.div(g, F // 2)
        value = xr[g].reshape(acc.shape[1], 2 * C)
        at = pl.ds(pl.multiple_of(f * 2 * C, 2 * C), 2 * C)
        width = min(lat, 256)

        @pl.loop(0, lat // width)
        def _(n):
            cols = pl.ds(pl.multiple_of(n * width, width), width)
            acc[stream, :, cols] += dot(value, enc[at, cols])

    def decode(g):
        f, stream = lax.rem(g, F // 2), lax.div(g, F // 2)
        at = pl.ds(pl.multiple_of(f * 2 * C, 2 * C), 2 * C)
        ys[g] = dot(act[stream], dec[:, at]).astype(BF16).reshape(NX, NS, 2 * C)

    def slots(f, g):
        return part_of(f, g, 0, NP)[...].reshape(NS, C)

    def within(n, count):
        return (n >= 0) & (n < count)

    encoding = 3 * HOP + SWAP
    later = F + GAP
    home = max(later + F - EARLY, later + encoding + PARTS)
    ending = SWAP + 3 * HOP

    @pl.loop(0, home + 2 * F + ending)
    def _(k):
        own = k - core * later

        def depart(f):
            cols = pl.ds(pl.multiple_of(f * C, C), C)
            cen[f] = (tok[:, cols].astype(F32) - dbias[:, cols]).astype(BF16)
            for w in range(2):
                hop(0, w, f).start()

        @pl.when(own == 0)
        def _():
            for f in range(LEAD):
                depart(f)

        @pl.when((own >= 0) & (own + LEAD < F))
        def _():
            depart(own + LEAD)

        @pl.when(k == HOP + 1)
        def _():
            bias = ebias[...] * jnp.where(y == 0, 1.0, 0.0)
            for stream in range(CORES):
                acc[stream] = jnp.broadcast_to(bias, acc.shape[1:])

        @pl.when(k == 0)
        def _():
            build_meta()
            for w in range(2):
                tgt_hop(0, w).start()
                meta_hop(0, w).start()
            kinds = placing(tgt[...], z, 0, NS)
            put(pown, tpown, 0, kinds)
            to_peers(ms, 0, pick_rows(kinds, meta[...]))

        @pl.when(within(own - HOP, F))
        def _():
            hop_landed(0, own - HOP)
            for w in range(2):
                hop(1, w, own - HOP).start()

        @pl.when(k == HOP)
        def _():
            for w in range(2):
                tgt_hop(0, w).wait_recv()
                meta_hop(0, w).wait_recv()
                tgt_hop(1, w).start()
                meta_hop(1, w).start()
                kinds = placing(tgt1[w], z, 0, NS)
                put(pone.at[w], tpone.at[w], 0, kinds)
                to_peers(ms, 1 + w, pick_rows(kinds, m1[w]))

        @pl.when(k == 2 * HOP)
        def _():
            for w in range(2):
                step = 1 - 2 * w
                tgt_hop(1, w).wait_recv()
                meta_hop(1, w).wait_recv()
                near = placing(tgt2[w], z, 0, NS)
                put(ptwo.at[w], tptwo.at[w], 0, near)
                to_peers(ms, 3 + w, pick_rows(near, m2[w]))
                far = placing(tgt2[w], plane_of(step), 0, NS)
                put(ptwo.at[w], tptwo.at[w], NS, far)
                m3s[w, 0:NS, :] = pick_rows(far, m2[w])
                last = placing(tgt2[w], plane_of(2 * step), HALF * w, HALF)
                put(ptwo.at[w], tptwo.at[w], 2 * NS, last)
                m3s[w, NS:NS + HALF, :] = pick_rows(last, m2[w])
                meta_hop(2, w).start()
                meta_hop(3, w).start()

        @pl.when(within(own - 2 * HOP, F))
        def _():
            f = own - 2 * HOP
            hop_landed(1, f)
            for w in range(2):
                two = dot(ptwo[w], r2[f, w]).astype(BF16)
                s3[w, f] = two[NS:, :]
                hop(2, w, f).start()
                hop(3, w, f).start()
                to_pair(f, 3 + w, two[0:NS, :])

        @pl.when(within(own - 3 * HOP, F))
        def _():
            f = own - 3 * HOP
            hop_landed(2, f)
            hop_landed(3, f)
            for w in range(2):
                to_pair(f, 5 + w, r3[f, w])
            to_pair(f, 7, jnp.concatenate([r4[f, 0], r4[f, 1]], axis=0))

            @pl.when(lax.rem(f, 2) == 1)
            def _():
                outward(core * (F // 2) + lax.div(f, 2)).start()

        @pl.when(k == 3 * HOP)
        def _():
            for w in range(2):
                meta_hop(2, w).wait_recv()
                meta_hop(3, w).wait_recv()
                to_peers(ms, 5 + w, m3[w])
            to_peers(ms, 7, jnp.concatenate([m4[0], m4[1]], axis=0))
            outward_meta(core).start()

        @pl.when(within(own - 2 * HOP, F))
        def _():
            f = own - 2 * HOP
            to_pair(f, 0, dot(pown[...], cen[f]).astype(BF16))
            for w in range(2):
                to_pair(f, 1 + w, dot(pone[w], r1[f, w]).astype(BF16))

        done = k - home - core * F

        @pl.when(within(done - SWAP - 2 * HOP, F))
        def _():
            f = done - SWAP - 2 * HOP
            back_landed(1, f)
            for w in range(2):
                part = dot(tpone[w], slots(f, 1 + w))
                b1[w, f] = (part + t2[f, w].astype(F32)).astype(BF16)
                back(0, w, f).start()

        @pl.when(within(done - SWAP - HOP, F))
        def _():
            f = done - SWAP - HOP
            back_landed(2, f)
            back_landed(3, f)
            for w in range(2):
                every = jnp.concatenate([slots(f, 3 + w), t3[f, w], t4[f, w]], axis=0)
                part = dot(tptwo[w, :, 0:2 * NS + HALF], every)
                b2[w, f] = part.astype(BF16)
                back(1, w, f).start()

        @pl.when(within(done - SWAP, F))
        def _():
            f = done - SWAP

            @pl.when(lax.rem(f, 2) == 0)
            def _():
                homeward_wait_recv(lax.div(f, 2))
            last = slots(f, 7)
            for w in range(2):
                b4[w, f] = last[HALF * w:HALF * (w + 1), :]
                back(3, w, f).start()
                b3[w, f] = slots(f, 5 + w)
                back(2, w, f).start()

        @pl.when(k == 3 * HOP)
        def _():
            enc_copy.wait()
            dec_copy.wait()

        for stream in range(CORES):
            ready = k - encoding - stream * later

            @pl.when(within(ready, F) & (lax.rem(ready, 2) == 1))
            def _():
                g = lax.div(ready, 2) + stream * (F // 2)
                outward(g).wait_recv(stream)
                encode(g)

        for stream in range(CORES):
            @pl.when(k == encoding + stream)
            def _():
                outward_meta(stream).wait_recv(stream)
                read_picks(stream)

        second = jnp.where(k >= later + F + encoding - 1, 1, 0)
        turn_step = k - (F + encoding - 1) - second * later

        @pl.when(within(turn_step, PARTS))
        def _():
            pick_values(second, turn_step)
            for turn in range(1, Y):
                y_copy(turn, second, turn_step).start()

        @pl.when(within(turn_step - 2, PARTS))
        def _():
            for turn in range(1, Y):
                y_copy(turn, second, turn_step - 2).wait_recv()
            spread_values(second, turn_step - 2)

        @pl.when(within(k - home, 2 * F) & (lax.rem(k - home, 2) == 0))
        def _():
            g = lax.div(k - home, 2)
            decode(g)
            homeward_start(g)

        @pl.when(within(done - ending, F))
        def _():
            f = done - ending
            whole = dot(tpown[...], slots(f, 0))
            back_landed(0, f)
            for w in range(2):
                whole = whole + t1[f, w].astype(F32)
            cols = pl.ds(pl.multiple_of(f * C, C), C)
            out[:, cols] = (whole + dbias[:, cols]).astype(BF16)

    def sent(ref, sem):
        pltpu.make_async_remote_copy(
            src_ref=ref, dst_ref=ref, send_sem=sem, recv_sem=mq_sem.at[0, 0],
            device_id=to_peer(1)[1], device_id_type=MESH,
        ).wait_send()

    for w in range(2):
        for h, ref in enumerate((cen, r1.at[:, w], r3.at[:, w], r4.at[:, w])):
            sent(ref, hs.at[h, w])
        for h, ref in enumerate((b1.at[w], b2.at[w], b3.at[w], b4.at[w])):
            sent(ref, us.at[h, w])
    sent(xs.at[:, pl.ds(0, NP - 1)], xs_sem.at[0])
    sent(yr.at[:, pl.ds(0, NP - 1)], vs_sem.at[0])
    for w in range(2):
        for h in range(4):
            meta_hop(h, w).wait_send()
        for h in range(2):
            tgt_hop(h, w).wait_send()
    sent(ms.at[pl.ds(0, NP - 1)], mx_sem.at[0])
    for stream in range(CORES):
        for half in range(PARTS):
            for turn in range(1, Y):
                y_copy(turn, stream, half).wait_send()


def on_device(tokens, dec_bias, routes, latent_picks, enc_weight, dec_weight, enc_bias):
    rows, width = tokens.shape
    lat = enc_weight.shape[2]
    Y = lax.axis_size("dp")
    nblk = lax.axis_size("blocks")
    NP = nblk // RING
    NX = NP // CORES
    NS = NP * CAP
    HALF = NS // 2
    F = CHUNKS
    C = width // F
    piece = GROUPS * CAP
    n = NX * piece
    vals = n // 128 * CAP
    V = pltpu.VMEM
    D = pltpu.SemaphoreType.DMA
    scratch = [
        V((width, lat), BF16), V((lat, width), BF16),
        V((F, rows, C), BF16), V((F, 2, rows, C), BF16), V((F, 2, rows, C), BF16),
        V((2, F, NS + HALF, C), BF16), V((F, 2, NS, C), BF16), V((F, 2, HALF, C), BF16),
        V((F // 2, NP, piece, 2 * C), BF16), V((CORES * (F // 2), NX, piece, 2 * C), BF16),
        V((CORES, n, lat), F32), V((CORES, n, lat), BF16),
        V((CORES * (F // 2), NX, piece, 2 * C), BF16), V((F // 2, NP, piece, 2 * C), BF16),
        V((2, F, HALF, C), BF16), V((2, F, NS, C), BF16),
        V((2, F, rows, C), BF16), V((2, F, rows, C), BF16),
        V((F, 2, HALF, C), BF16), V((F, 2, NS, C), BF16),
        V((F, 2, rows, C), BF16), V((F, 2, rows, C), BF16),
        V((NS, rows), BF16), V((2, NS, rows), BF16), V((2, 2 * NS + HALF, rows), BF16),
        V((rows, NS), BF16), V((2, rows, NS), BF16), V((2, rows, 3 * NS), BF16),
        V((8, rows), F32), V((2, 8, rows), F32), V((2, 8, rows), F32),
        V((rows, 128), BF16), V((2, rows, 128), BF16), V((2, rows, 128), BF16),
        V((2, NS + HALF, 128), BF16), V((2, NS, 128), BF16), V((2, HALF, 128), BF16),
        V((NP, piece, 128), BF16), V((CORES, NX, piece, 128), BF16),
        V((CORES, n, 128), jnp.int32), V((CORES, vals, 128), F32),
        V((CORES, max(Y - 1, 1), vals, 128), F32),
        D((2,)), D((4, 2)), D((4, F)), D((4, 2)), D((4, F)),
        D((1,)), D((F,)), D((F // 2,)), D((1,)), D((F // 2,)), D((F // 2,)),
        D((6, 2)), D((6, 2)), D((2,)), D((CORES,)),
        D((CORES, PARTS, max(Y - 1, 1))), D((CORES, PARTS, max(Y - 1, 1))),
    ]
    vmem = pl.BlockSpec(memory_space=pltpu.VMEM)
    hbm = pl.BlockSpec(memory_space=pl.ANY)
    return pl.pallas_call(
        kernel,
        out_shape=jax.ShapeDtypeStruct((rows, width), BF16),
        in_specs=[vmem] * 5 + [hbm] * 2,
        out_specs=vmem,
        scratch_shapes=scratch,
        compiler_params=pltpu.CompilerParams(
            collective_id=0, has_side_effects=True, vmem_limit_bytes=63 * 1024 * 1024
        ),
    )(
        tokens, dec_bias.reshape(1, width), routes.T,
        latent_picks.transpose(1, 2, 0).reshape(-1, rows), enc_bias, enc_weight, dec_weight,
    )


def solution(mesh):
    in_specs = (
        P("blocks", "dp"),
        P("dp"),
        P("blocks", None),
        P("blocks", None, None),
        P("blocks", "dp", None),
        P("blocks", None, "dp"),
        P("blocks", None),
    )
    return jax.shard_map(
        on_device, mesh=mesh, in_specs=in_specs, out_specs=P("blocks", "dp"), check_vma=False
    )
```

```python
import functools

import jax
import jax.numpy as jnp
from jax import lax
from jax.experimental import pallas as pl
from jax.experimental.pallas import tpu as pltpu
from jax.sharding import PartitionSpec as P

F32 = jnp.float32
BF16 = jnp.bfloat16
MESH = pl.DeviceIdType.MESH
RING = 8
CORES = 2
CAP = 16
CHUNKS = 16
HOP = 3
LEAD = 2
FIRST = 1
GAP = 0
EARLY = 4
SWAP = 3
PARTS = 2
GROUPS = 8


def dot(a, b):
    return jnp.dot(a, b, preferred_element_type=F32)


def iota(shape, axis):
    return lax.broadcasted_iota(jnp.int32, shape, axis)


def kernel(
    tok, dbias, routes, picks, ebias, enc_hbm, dec_hbm, out,
    enc, dec, cen, r1, r2, s3, r3, r4, xs, xr, acc, act, ys, yr,
    b4, b3, b2, b1, t4, t3, t2, t1,
    pown, pone, ptwo, tpown, tpone, tptwo,
    tgt, tgt1, tgt2, meta, m1, m2, m3s, m3, m4, ms, mr, idx, yv, yg,
    wsem, hs, hq, us, uq, xs_sem, xq_sem, xl_sem, vs_sem, vq_sem, vl_sem,
    ms_sem, mq_sem, mx_sem, mr_sem, ysem_s, ysem_q,
):
    rows = tok.shape[0]
    F, _, C = cen.shape
    NP = xs.shape[1]
    NX = NP // CORES
    NS = NP * CAP
    HALF = NS // 2
    top = routes.shape[0]
    lat = enc.shape[1]
    Y = lax.axis_size("dp")

    y = lax.axis_index("dp")
    b = lax.axis_index("blocks")
    core = lax.rem(b, CORES)
    z = lax.rem(lax.div(b, CORES), RING)
    x = lax.div(b, CORES * RING)
    me = x * CORES + core

    def block_of(p, plane):
        return (lax.div(p, CORES) * RING + plane) * CORES + lax.rem(p, CORES)

    def plane_of(step):
        return lax.rem(z + step + RING, RING)

    ahead = (block_of(me, plane_of(1)), block_of(me, plane_of(-1)))
    beyond = (block_of(me, plane_of(2)), block_of(me, plane_of(-2)))

    def to_peer(turn):
        p = lax.rem(me + turn, NP)
        return p, (y, block_of(p, z))

    def z_copy(src, dst, ssem, rsem, way, far=False):
        return pltpu.make_async_remote_copy(
            src_ref=src, dst_ref=dst, send_sem=ssem, recv_sem=rsem,
            device_id=(y, (beyond if far else ahead)[way]), device_id_type=MESH,
        )

    barrier = pltpu.get_barrier_semaphore()
    for way in range(2):
        pl.semaphore_signal(barrier, inc=1, device_id=(y, ahead[way]), device_id_type=MESH)
        pl.semaphore_signal(barrier, inc=1, device_id=(y, beyond[way]), device_id_type=MESH)
    for turn in range(1, NP):
        pl.semaphore_signal(barrier, inc=1, device_id=to_peer(turn)[1], device_id_type=MESH)
    for turn in range(1, Y):
        pl.semaphore_signal(
            barrier, inc=1, device_id=(lax.rem(y + turn, Y), b), device_id_type=MESH
        )
    enc_copy = pltpu.make_async_copy(enc_hbm.at[0], enc, wsem.at[0])
    dec_copy = pltpu.make_async_copy(dec_hbm.at[0], dec, wsem.at[1])
    enc_copy.start()
    dec_copy.start()
    pl.semaphore_wait(barrier, 4 + NP - 1 + Y - 1)

    def hop(h, w, f):
        src, dst = (
            (cen.at[f], r1.at[f, w]),
            (r1.at[f, w], r2.at[f, w]),
            (s3.at[w, f, pl.ds(0, NS)], r3.at[f, w]),
            (s3.at[w, f, pl.ds(NS, HALF)], r4.at[f, w]),
        )[h]
        return z_copy(src, dst, hs.at[h, w], hq.at[h, f], w, h == 3)

    def landed(ref, sem):
        pltpu.make_async_remote_copy(
            src_ref=ref, dst_ref=ref, send_sem=mq_sem.at[0, 0], recv_sem=sem,
            device_id=to_peer(1)[1], device_id_type=MESH,
        ).wait_recv()

    def hop_landed(h, f):
        landed((r1, r2, r3, r4)[h].at[f], hq.at[h, f])

    def back_landed(h, f):
        landed((t1, t2, t3, t4)[h].at[f], uq.at[h, f])

    def half_cols(f):
        return pl.ds(pl.multiple_of(lax.rem(f, 2) * C, C), C)

    def part_of(f, g, p, n):
        return yr.at[lax.div(f, 2), pl.ds(p, n), pl.ds(g * CAP, CAP), half_cols(f)]

    def back(h, w, f):
        src, dst = (
            (b1.at[w, f], t1.at[f, w]),
            (b2.at[w, f], t2.at[f, w]),
            (b3.at[w, f], t3.at[f, w]),
            (b4.at[w, f], t4.at[f, w]),
        )[h]
        return z_copy(src, dst, us.at[h, w], uq.at[h, f], 1 - w, h == 3)

    def meta_hop(h, w):
        src, dst = (
            (meta, m1.at[w]),
            (m1.at[w], m2.at[w]),
            (m3s.at[w, pl.ds(0, NS)], m3.at[w]),
            (m3s.at[w, pl.ds(NS, HALF)], m4.at[w]),
        )[h]
        return z_copy(src, dst, ms_sem.at[h, w], mq_sem.at[h, w], w, h == 3)

    def tgt_hop(h, w):
        src, dst = ((tgt, tgt1.at[w]), (tgt1.at[w], tgt2.at[w]))[h]
        return z_copy(src, dst, ms_sem.at[4 + h, w], mq_sem.at[4 + h, w], w)

    class Outward:
        def __init__(self, send, landing, ssem, rsem, lsem):
            self.send, self.landing, self.sems = send, landing, (ssem, rsem, lsem)

        def local(self):
            return pltpu.make_async_copy(self.send.at[me], self.landing.at[x], self.sems[2])

        def start(self):
            for turn in range(1, NP):
                p, device = to_peer(turn)
                pltpu.make_async_remote_copy(
                    src_ref=self.send.at[p], dst_ref=self.landing.at[x],
                    send_sem=self.sems[0], recv_sem=self.sems[1],
                    device_id=device, device_id_type=MESH,
                ).start()
            self.local().start()

        def wait_recv(self, stream):
            def pieces(n):
                pltpu.make_async_remote_copy(
                    src_ref=self.landing.at[pl.ds(0, n)], dst_ref=self.landing.at[pl.ds(0, n)],
                    send_sem=self.sems[0], recv_sem=self.sems[1],
                    device_id=to_peer(1)[1], device_id_type=MESH,
                ).wait_recv()

            @pl.when(stream == core)
            def _():
                if NX > 1:
                    pieces(NX - 1)
                self.local().wait()

            @pl.when(stream != core)
            def _():
                pieces(NX)

    def outward(g):
        f = lax.rem(g, F // 2)
        return Outward(xs.at[f], xr.at[g], xs_sem.at[0], xq_sem.at[g], xl_sem.at[f])

    def outward_meta(stream):
        return Outward(ms, mr.at[stream], mx_sem.at[0], mr_sem.at[stream], mx_sem.at[1])

    def homeward(g, turn):
        f, stream = lax.rem(g, F // 2), lax.div(g, F // 2)
        to = lax.rem(x + turn, NX)
        p = to * CORES + stream
        return pltpu.make_async_remote_copy(
            src_ref=ys.at[g, to], dst_ref=yr.at[f, me],
            send_sem=vs_sem.at[0], recv_sem=vq_sem.at[f],
            device_id=(y, block_of(p, z)), device_id_type=MESH,
        )

    def homeward_local(g):
        f = lax.rem(g, F // 2)
        return pltpu.make_async_copy(ys.at[g, x], yr.at[f, me], vl_sem.at[f])

    def homeward_start(g):
        stream = lax.div(g, F // 2)
        for turn in range(1, NX):
            homeward(g, turn).start()

        @pl.when(stream == core)
        def _():
            homeward_local(g).start()

        @pl.when(stream != core)
        def _():
            homeward(g, 0).start()

    def homeward_wait_recv(f):
        pltpu.make_async_remote_copy(
            src_ref=yr.at[f, pl.ds(0, NP - 1)], dst_ref=yr.at[f, pl.ds(0, NP - 1)],
            send_sem=vs_sem.at[0], recv_sem=vq_sem.at[f],
            device_id=to_peer(1)[1], device_id_type=MESH,
        ).wait_recv()
        homeward_local(core * (F // 2) + f).wait()

    part_rows = acc.shape[1] // PARTS
    part_vals = part_rows // 128 * CAP

    def y_copy(turn, stream, half):
        at = pl.ds(half * part_vals, part_vals)
        return pltpu.make_async_remote_copy(
            src_ref=yv.at[stream, at], dst_ref=yg.at[stream, turn - 1, at],
            send_sem=ysem_s.at[stream, half, turn - 1], recv_sem=ysem_q.at[stream, half, turn - 1],
            device_id=(lax.rem(y + turn, Y), b), device_id_type=MESH,
        )

    def placing(targets, plane, first, count):
        q = iota((count, rows), 0) + first
        ids = ((lax.shift_right_logical(q, 5) * RING + plane) * CORES
               + (lax.shift_right_logical(q, 4) & 1)) * CAP + (q & (CAP - 1))
        ids = ids.astype(F32)
        return [jnp.where(targets[k:k + 1, :] == ids, 1.0, 0.0) for k in range(top)]

    def put(p_ref, t_ref, lo, kinds):
        whole = kinds[0]
        for other in kinds[1:]:
            whole = whole + other
        n = whole.shape[0]
        p_ref[lo:lo + n, :] = whole.astype(BF16)
        t_ref[:, lo:lo + n] = whole.T.astype(BF16)

    def pick_rows(kinds, source):
        total = None
        for k, one in enumerate(kinds):
            part = dot(one.astype(BF16), source).astype(BF16)
            take = (iota((128, 128), 0) == iota((128, 128), 1) + 32 * k) & (iota((128, 128), 1) < 32)
            part = dot(part, jnp.where(take, 1.0, 0.0).astype(BF16))
            total = part if total is None else total + part
        return total.astype(BF16)

    def to_pair(f, g, value):
        to_peers(xs.at[lax.div(f, 2), :, :, half_cols(f)], g, value)

    def to_peers(ref, g, value):
        ref[:, g * CAP:(g + 1) * CAP, :] = value.reshape(NP, CAP, value.shape[-1])

    def build_meta():
        tgt[...] = jnp.zeros(tgt.shape, F32)
        before = jnp.where(iota((rows, rows), 0) < iota((rows, rows), 1), 1.0, 0.0).astype(BF16)
        so_far = jnp.zeros((128, 1), F32)
        for k in range(top):
            owner = routes[k:k + 1, :]
            named = jnp.where(owner == iota((128, rows), 0), 1.0, 0.0)
            rank = jnp.sum(named * (dot(named.astype(BF16), before) + so_far), axis=0, keepdims=True)
            so_far = so_far + jnp.sum(named, axis=1, keepdims=True)
            tgt[k:k + 1, :] = owner.astype(F32) * CAP + rank
        chosen = picks[...]
        n = chosen.shape[0]
        lane, col = iota((128, n), 0), iota((128, n), 1)
        base = lax.shift_right_logical(col, 4) * 32 + (col & 15)
        hi = lax.shift_right_logical(chosen, 3).astype(F32).astype(BF16)
        lo = (chosen & 7).astype(F32).astype(BF16)
        meta[...] = (
            dot(jnp.where(lane == base, 1.0, 0.0).astype(BF16), hi)
            + dot(jnp.where(lane == base + 16, 1.0, 0.0).astype(BF16), lo)
        ).T.astype(BF16)

    def pick_values(stream, half):
        @pl.loop(0, part_rows // 128)
        def _(i):
            j = half * (part_rows // 128) + i
            at = pl.ds(pl.multiple_of(j * 128, 128), 128)
            ids = idx[stream, at, :]
            got = jnp.zeros((128, 128), F32)
            for tile in range(lat // 128):
                here = jnp.take_along_axis(
                    acc[stream, at, tile * 128:(tile + 1) * 128], ids & 127, axis=1,
                    mode="promise_in_bounds",
                )
                got = jnp.where(lax.shift_right_logical(ids, 7) == tile, here, got)
            yv[stream, pl.ds(pl.multiple_of(j * CAP, CAP), CAP), :] = got.T[0:CAP, :]

    def spread_values(stream, half):
        @pl.loop(0, part_rows // 128)
        def _(i):
            j = half * (part_rows // 128) + i
            small = pl.ds(pl.multiple_of(j * CAP, CAP), CAP)
            value = yv[stream, small, :]
            for turn in range(1, Y):
                value = value + yg[stream, turn - 1, small, :]
            value = jnp.maximum(value, 0.0)
            value = jnp.concatenate([value, jnp.zeros((128 - CAP, 128), F32)], axis=0).T
            ids = idx[stream, pl.ds(pl.multiple_of(j * 128, 128), 128), :]
            lane = iota((32, lat), 1)
            for part in range(4):
                sub = slice(part * 32, (part + 1) * 32)
                full = jnp.zeros((32, lat), F32)
                for i in range(CAP):
                    full = jnp.where(lane == ids[sub, i:i + 1], value[sub, i:i + 1], full)
                at = pl.ds(pl.multiple_of(j * 128 + part * 32, 32), 32)
                act[stream, at, :] = full.astype(BF16)

    def read_picks(stream):
        one = mr[stream].reshape(acc.shape[1], 128)
        j, i = iota((128, 128), 0), iota((128, 128), 1)
        weigh = jnp.where(j == i, 8.0, jnp.where(j == i + 16, 1.0, 0.0))
        weigh = jnp.where(i < 16, weigh, 0.0).astype(BF16)
        idx[stream] = dot(one, weigh).astype(jnp.int32)

    def encode(g):
        f, stream = lax.rem(g, F // 2), lax.div(g, F // 2)
        value = xr[g].reshape(acc.shape[1], 2 * C)
        at = pl.ds(pl.multiple_of(f * 2 * C, 2 * C), 2 * C)
        width = min(lat, 256)

        @pl.loop(0, lat // width)
        def _(n):
            cols = pl.ds(pl.multiple_of(n * width, width), width)
            acc[stream, :, cols] += dot(value, enc[at, cols])

    def decode(g):
        f, stream = lax.rem(g, F // 2), lax.div(g, F // 2)
        at = pl.ds(pl.multiple_of(f * 2 * C, 2 * C), 2 * C)
        ys[g] = dot(act[stream], dec[:, at]).astype(BF16).reshape(NX, NS, 2 * C)

    def slots(f, g):
        return part_of(f, g, 0, NP)[...].reshape(NS, C)

    def within(n, count):
        return (n >= 0) & (n < count)

    encoding = FIRST + 2 * HOP + SWAP
    later = F + GAP
    home = max(later + F - EARLY, later + encoding + PARTS)
    ending = SWAP + 3 * HOP

    @pl.loop(0, home + 2 * F + ending)
    def _(k):
        own = k - core * later

        def depart(f):
            cols = pl.ds(pl.multiple_of(f * C, C), C)
            cen[f] = (tok[:, cols].astype(F32) - dbias[:, cols]).astype(BF16)
            for w in range(2):
                hop(0, w, f).start()

        @pl.when(own == 0)
        def _():
            for f in range(LEAD):
                depart(f)

        @pl.when((own >= 0) & (own + LEAD < F))
        def _():
            depart(own + LEAD)

        @pl.when(k == 3)
        def _():
            bias = ebias[...] * jnp.where(y == 0, 1.0, 0.0)
            for stream in range(CORES):
                acc[stream] = jnp.broadcast_to(bias, acc.shape[1:])

        @pl.when(k == 0)
        def _():
            build_meta()
            for w in range(2):
                tgt_hop(0, w).start()
                meta_hop(0, w).start()
            kinds = placing(tgt[...], z, 0, NS)
            put(pown, tpown, 0, kinds)
            to_peers(ms, 0, pick_rows(kinds, meta[...]))

        @pl.when(within(own - FIRST, F))
        def _():
            hop_landed(0, own - FIRST)
            for w in range(2):
                hop(1, w, own - FIRST).start()

        @pl.when(k == 2)
        def _():
            for w in range(2):
                tgt_hop(0, w).wait_recv()
                meta_hop(0, w).wait_recv()
                tgt_hop(1, w).start()
                meta_hop(1, w).start()
                kinds = placing(tgt1[w], z, 0, NS)
                put(pone.at[w], tpone.at[w], 0, kinds)
                to_peers(ms, 1 + w, pick_rows(kinds, m1[w]))

        @pl.when(k == FIRST + HOP)
        def _():
            for w in range(2):
                step = 1 - 2 * w
                tgt_hop(1, w).wait_recv()
                meta_hop(1, w).wait_recv()
                near = placing(tgt2[w], z, 0, NS)
                put(ptwo.at[w], tptwo.at[w], 0, near)
                to_peers(ms, 3 + w, pick_rows(near, m2[w]))
                far = placing(tgt2[w], plane_of(step), 0, NS)
                put(ptwo.at[w], tptwo.at[w], NS, far)
                m3s[w, 0:NS, :] = pick_rows(far, m2[w])
                last = placing(tgt2[w], plane_of(2 * step), HALF * w, HALF)
                put(ptwo.at[w], tptwo.at[w], 2 * NS, last)
                m3s[w, NS:NS + HALF, :] = pick_rows(last, m2[w])
                meta_hop(2, w).start()
                meta_hop(3, w).start()

        @pl.when(within(own - FIRST - HOP, F))
        def _():
            f = own - FIRST - HOP
            hop_landed(1, f)
            for w in range(2):
                two = dot(ptwo[w], r2[f, w]).astype(BF16)
                s3[w, f] = two[NS:, :]
                hop(2, w, f).start()
                hop(3, w, f).start()
                to_pair(f, 3 + w, two[0:NS, :])

        @pl.when(within(own - FIRST - 2 * HOP, F))
        def _():
            f = own - FIRST - 2 * HOP
            hop_landed(2, f)
            hop_landed(3, f)
            for w in range(2):
                to_pair(f, 5 + w, r3[f, w])
            to_pair(f, 7, jnp.concatenate([r4[f, 0], r4[f, 1]], axis=0))

            @pl.when(lax.rem(f, 2) == 1)
            def _():
                outward(core * (F // 2) + lax.div(f, 2)).start()

        @pl.when(k == FIRST + 2 * HOP)
        def _():
            for w in range(2):
                meta_hop(2, w).wait_recv()
                meta_hop(3, w).wait_recv()
                to_peers(ms, 5 + w, m3[w])
            to_peers(ms, 7, jnp.concatenate([m4[0], m4[1]], axis=0))
            outward_meta(core).start()

        @pl.when(within(own - FIRST - HOP, F))
        def _():
            f = own - FIRST - HOP
            to_pair(f, 0, dot(pown[...], cen[f]).astype(BF16))
            for w in range(2):
                to_pair(f, 1 + w, dot(pone[w], r1[f, w]).astype(BF16))

        done = k - home - core * F

        @pl.when(within(done - SWAP - 2 * HOP, F))
        def _():
            f = done - SWAP - 2 * HOP
            back_landed(1, f)
            for w in range(2):
                part = dot(tpone[w], slots(f, 1 + w))
                b1[w, f] = (part + t2[f, w].astype(F32)).astype(BF16)
                back(0, w, f).start()

        @pl.when(within(done - SWAP - HOP, F))
        def _():
            f = done - SWAP - HOP
            back_landed(2, f)
            back_landed(3, f)
            for w in range(2):
                every = jnp.concatenate([slots(f, 3 + w), t3[f, w], t4[f, w]], axis=0)
                part = dot(tptwo[w, :, 0:2 * NS + HALF], every)
                b2[w, f] = part.astype(BF16)
                back(1, w, f).start()

        @pl.when(within(done - SWAP, F))
        def _():
            f = done - SWAP

            @pl.when(lax.rem(f, 2) == 0)
            def _():
                homeward_wait_recv(lax.div(f, 2))
            last = slots(f, 7)
            for w in range(2):
                b4[w, f] = last[HALF * w:HALF * (w + 1), :]
                back(3, w, f).start()
                b3[w, f] = slots(f, 5 + w)
                back(2, w, f).start()

        @pl.when(k == 3 * HOP)
        def _():
            enc_copy.wait()
            dec_copy.wait()

        for stream in range(CORES):
            ready = k - encoding - stream * later

            @pl.when(within(ready, F) & (lax.rem(ready, 2) == 1))
            def _():
                g = lax.div(ready, 2) + stream * (F // 2)
                outward(g).wait_recv(stream)
                encode(g)

        for stream in range(CORES):
            @pl.when(k == encoding + stream)
            def _():
                outward_meta(stream).wait_recv(stream)
                read_picks(stream)

        second = jnp.where(k >= later + F + encoding - 1, 1, 0)
        turn_step = k - (F + encoding - 1) - second * later

        @pl.when(within(turn_step, PARTS))
        def _():
            pick_values(second, turn_step)
            for turn in range(1, Y):
                y_copy(turn, second, turn_step).start()

        @pl.when(within(turn_step - 2, PARTS))
        def _():
            for turn in range(1, Y):
                y_copy(turn, second, turn_step - 2).wait_recv()
            spread_values(second, turn_step - 2)

        @pl.when(within(k - home, 2 * F) & (lax.rem(k - home, 2) == 0))
        def _():
            g = lax.div(k - home, 2)
            decode(g)
            homeward_start(g)

        @pl.when(within(done - ending, F))
        def _():
            f = done - ending
            whole = dot(tpown[...], slots(f, 0))
            back_landed(0, f)
            for w in range(2):
                whole = whole + t1[f, w].astype(F32)
            cols = pl.ds(pl.multiple_of(f * C, C), C)
            out[:, cols] = (whole + dbias[:, cols]).astype(BF16)

    def sent(ref, sem):
        pltpu.make_async_remote_copy(
            src_ref=ref, dst_ref=ref, send_sem=sem, recv_sem=mq_sem.at[0, 0],
            device_id=to_peer(1)[1], device_id_type=MESH,
        ).wait_send()

    for w in range(2):
        for h, ref in enumerate((cen, r1.at[:, w], r3.at[:, w], r4.at[:, w])):
            sent(ref, hs.at[h, w])
        for h, ref in enumerate((b1.at[w], b2.at[w], b3.at[w], b4.at[w])):
            sent(ref, us.at[h, w])
    sent(xs.at[:, pl.ds(0, NP - 1)], xs_sem.at[0])
    sent(yr.at[:, pl.ds(0, NP - 1)], vs_sem.at[0])
    for w in range(2):
        for h in range(4):
            meta_hop(h, w).wait_send()
        for h in range(2):
            tgt_hop(h, w).wait_send()
    sent(ms.at[pl.ds(0, NP - 1)], mx_sem.at[0])
    for stream in range(CORES):
        for half in range(PARTS):
            for turn in range(1, Y):
                y_copy(turn, stream, half).wait_send()


def on_device(tokens, dec_bias, routes, latent_picks, enc_weight, dec_weight, enc_bias):
    rows, width = tokens.shape
    lat = enc_weight.shape[2]
    Y = lax.axis_size("dp")
    nblk = lax.axis_size("blocks")
    NP = nblk // RING
    NX = NP // CORES
    NS = NP * CAP
    HALF = NS // 2
    F = CHUNKS
    C = width // F
    piece = GROUPS * CAP
    n = NX * piece
    vals = n // 128 * CAP
    V = pltpu.VMEM
    D = pltpu.SemaphoreType.DMA
    scratch = [
        V((width, lat), BF16), V((lat, width), BF16),
        V((F, rows, C), BF16), V((F, 2, rows, C), BF16), V((F, 2, rows, C), BF16),
        V((2, F, NS + HALF, C), BF16), V((F, 2, NS, C), BF16), V((F, 2, HALF, C), BF16),
        V((F // 2, NP, piece, 2 * C), BF16), V((CORES * (F // 2), NX, piece, 2 * C), BF16),
        V((CORES, n, lat), F32), V((CORES, n, lat), BF16),
        V((CORES * (F // 2), NX, piece, 2 * C), BF16), V((F // 2, NP, piece, 2 * C), BF16),
        V((2, F, HALF, C), BF16), V((2, F, NS, C), BF16),
        V((2, F, rows, C), BF16), V((2, F, rows, C), BF16),
        V((F, 2, HALF, C), BF16), V((F, 2, NS, C), BF16),
        V((F, 2, rows, C), BF16), V((F, 2, rows, C), BF16),
        V((NS, rows), BF16), V((2, NS, rows), BF16), V((2, 2 * NS + HALF, rows), BF16),
        V((rows, NS), BF16), V((2, rows, NS), BF16), V((2, rows, 3 * NS), BF16),
        V((8, rows), F32), V((2, 8, rows), F32), V((2, 8, rows), F32),
        V((rows, 128), BF16), V((2, rows, 128), BF16), V((2, rows, 128), BF16),
        V((2, NS + HALF, 128), BF16), V((2, NS, 128), BF16), V((2, HALF, 128), BF16),
        V((NP, piece, 128), BF16), V((CORES, NX, piece, 128), BF16),
        V((CORES, n, 128), jnp.int32), V((CORES, vals, 128), F32),
        V((CORES, max(Y - 1, 1), vals, 128), F32),
        D((2,)), D((4, 2)), D((4, F)), D((4, 2)), D((4, F)),
        D((1,)), D((F,)), D((F // 2,)), D((1,)), D((F // 2,)), D((F // 2,)),
        D((6, 2)), D((6, 2)), D((2,)), D((CORES,)),
        D((CORES, PARTS, max(Y - 1, 1))), D((CORES, PARTS, max(Y - 1, 1))),
    ]
    vmem = pl.BlockSpec(memory_space=pltpu.VMEM)
    hbm = pl.BlockSpec(memory_space=pl.ANY)
    return pl.pallas_call(
        kernel,
        out_shape=jax.ShapeDtypeStruct((rows, width), BF16),
        in_specs=[vmem] * 5 + [hbm] * 2,
        out_specs=vmem,
        scratch_shapes=scratch,
        compiler_params=pltpu.CompilerParams(
            collective_id=0, has_side_effects=True, vmem_limit_bytes=63 * 1024 * 1024
        ),
    )(
        tokens, dec_bias.reshape(1, width), routes.T,
        latent_picks.transpose(1, 2, 0).reshape(-1, rows), enc_bias, enc_weight, dec_weight,
    )


def solution(mesh):
    in_specs = (
        P("blocks", "dp"),
        P("dp"),
        P("blocks", None),
        P("blocks", None, None),
        P("blocks", "dp", None),
        P("blocks", None, "dp"),
        P("blocks", None),
    )
    return jax.shard_map(
        on_device, mesh=mesh, in_specs=in_specs, out_specs=P("blocks", "dp"), check_vma=False
    )
```
